32 devices in a mesh: groups: 2 (over x), win: 4 (over y, core), rcv: 4 (over z).
Axes of the slice: x: 2, y: 2, z: 4, core: 2. Of those that a mesh axis runs over, the one named last changes fastest.
Arguments:
- traces: bfloat16 [32, 768, 4096], P('win', ('groups', 'rcv')), parts along dimension 1, may hold values from -6 to 6
- valid: int32 [64], P(('groups', 'win')), parts along dimension 0, may hold values 0 or 1
- src_station: int32 [64], P('groups'), parts along dimension 0, may hold values from 0 to 383, as said below
Outputs:
- stacks: float32 [32, 768, 2, 512], P(None, ('groups', 'rcv'), None, 'win'), parts along dimension 1
The draws below stay inside these ranges and needn't reach their ends.
There are 2 independent parts, one for each index of `groups`. The reference program is written for one: setup_inputs(seed, part) draws one part's arguments, and reference() takes and returns one part's arrays. A program takes and returns all parts, laid end to end along the dimension named above; each array names one. Nothing has to cross between parts.
Inputs may be any that keep to these rules, and one draw needn't show every extreme that they name: `src_station`: distinct stations; station 0 and station 384 - 1 are always among them.
All inputs are finite; a program needn't handle non-finite values. No bound on the sum of `valid` on one device may be relied on, other than what follows from the above.
Results may differ from the reference program's by a relative error of at most 0.0049.
Values may be sent and summed in bfloat16 or wider, within the bound.
A program may use at most 128 MiB of HBM per device.

```python
import math
import jax
import jax.numpy as jnp
from jax import lax

NT = 4096
F = 512
K0 = 256
SOURCES = 32
WINDOWS = 32
RECEIVERS = 384


def draw_src_station(key, part):
    inner = jax.random.permutation(key, RECEIVERS - 2)[:SOURCES - 2].astype(jnp.int32) + 1
    ends = jnp.array([0, RECEIVERS - 1], dtype=jnp.int32)
    picked = jnp.concatenate([ends, inner])
    return jax.random.permutation(jax.random.fold_in(key, 7), picked).astype(jnp.int32)


def place_ends(entries, rng, smallest, top_value):
    place = [jax.random.randint(jax.random.fold_in(rng, axis), (), 0, length) for axis, length in enumerate(entries.shape)]
    longest = entries.shape.index(max(entries.shape))
    beside = place[:longest] + [(place[longest] + 1) % entries.shape[longest]] + place[longest + 1:]
    return entries.at[tuple(place)].set(smallest).at[tuple(beside)].set(top_value)


def block_levels(key, dims, pieces, least, largest):
    def one(dim, shards_of):
        draws = jax.random.uniform(jax.random.fold_in(jax.random.fold_in(key, 6), dim), (shards_of,), jnp.float32, least / len(pieces), largest / len(pieces))
        return jnp.repeat(jnp.exp(draws), dims[dim] // shards_of).reshape((-1,) + (1,) * (len(dims) - dim - 1))

    factor_of = one(*pieces[0])
    for cut in pieces[1:]:
        factor_of = factor_of * one(*cut)
    return factor_of


def scatter_about(rng, dims, scale, bound, shards=(), kind=jnp.bfloat16):
    level = block_levels(rng, dims, shards, -0.22, 0.18) if shards else 1.0
    entries = jax.random.normal(rng, dims, jnp.float32) * scale * level
    return jnp.minimum(jnp.maximum(entries, -bound), bound).astype(kind)


def setup_inputs(seed: int = 0, part: int = 0) -> dict:
    key_of = jax.random.split(jax.random.key(seed), 4)
    own_keys = jax.random.split(jax.random.fold_in(key_of[3], part), 4)
    traces = scatter_about(own_keys[0], (WINDOWS, RECEIVERS, NT), 1.0, 6.0, ((0, 4), (1, 4)))
    valid = place_ends((jax.random.randint(own_keys[1], (WINDOWS,), 0, 4) < 3).astype(jnp.int32), jax.random.fold_in(own_keys[1], 1), 0, 1)
    src_station = draw_src_station(jax.random.fold_in(jax.random.fold_in(key_of[3], part), 71), part)
    return dict(traces=traces, valid=valid, src_station=src_station)


def band_table(count, bins, first):
    samples = jnp.arange(count, dtype=jnp.int32)
    freqs = first + jnp.arange(bins, dtype=jnp.int32)
    phase = samples[:, None] * freqs[None, :] % count
    angle = phase.astype(jnp.float32) * (2.0 * math.pi / count)
    return jnp.concatenate([jnp.cos(angle), -jnp.sin(angle)], axis=1).astype(jnp.bfloat16)

def reference(traces, valid, src_station):
    table = band_table(NT, F, K0)

    def whiten(window):
        spectra = jnp.dot(window, table, preferred_element_type=jnp.float32)
        spectra = spectra.reshape(window.shape[0], 2, F)
        power = lax.optimization_barrier(jnp.sum(spectra * spectra, axis=(1, 2), keepdims=True)) / F
        return (spectra * lax.rsqrt(power + 1e-06)).astype(jnp.bfloat16)
    white = lax.map(whiten, traces)
    received = white * valid.astype(jnp.bfloat16)[:, None, None, None]
    sources = white[:, src_station]
    rr = received[:, :, 0].astype(jnp.float32)
    ri = received[:, :, 1].astype(jnp.float32)
    sr = sources[:, :, 0].astype(jnp.float32)
    si = sources[:, :, 1].astype(jnp.float32)
    real = jnp.einsum('wsf,wrf->srf', sr, rr) + jnp.einsum('wsf,wrf->srf', si, ri)
    imag = jnp.einsum('wsf,wrf->srf', sr, ri) - jnp.einsum('wsf,wrf->srf', si, rr)
    return jnp.stack([real, imag], axis=2) * (1.0 / math.sqrt(WINDOWS))
```

```python
import functools
import math

import jax
import jax.numpy as jnp
import ml_dtypes
import numpy as np
from jax import lax
from jax.experimental import pallas as pl
from jax.experimental.pallas import tpu as pltpu
from jax.sharding import PartitionSpec as P

F = 512
BLOCK = 256
MM = 2
LAG = 1
HOP = (1, 2)
GRANT = 48
PAIR = 2
MESH = pl.DeviceIdType.MESH


def band_table(count, bins, first):
    samples = np.arange(count, dtype=np.int64)
    freqs = first + np.arange(bins, dtype=np.int64)
    phase = samples[:, None] * freqs[None, :] % count
    angle = phase.astype(np.float64) * (2.0 * math.pi / count)
    return np.concatenate([np.cos(angle), -np.sin(angle)], axis=1).astype(ml_dtypes.bfloat16)


def half_table(count, bins, first):
    table = band_table(count, bins, first)[: count // 2]
    return np.stack(np.split(table, 2 * bins // BLOCK, axis=1))


def plain_body(traces, valid, src_station):
    w_dev, r_dev, samples = traces.shape
    bins = F
    n_win = lax.axis_size("win")
    f_dev = bins // n_win
    table = jnp.asarray(band_table(samples, bins, samples // 16))
    spectra = jnp.dot(
        traces.reshape(w_dev * r_dev, samples), table, preferred_element_type=jnp.float32
    )
    power = jnp.sum(spectra * spectra, axis=1, keepdims=True) / bins
    keep = jnp.repeat(valid.astype(jnp.float32), r_dev)[:, None]
    white = (spectra * (lax.rsqrt(power + 1e-06) * keep)).astype(jnp.bfloat16)
    white = white.reshape(w_dev * r_dev, 2, n_win, f_dev)
    pieces = jnp.transpose(white, (2, 1, 0, 3))
    got = lax.all_to_all(pieces, "win", 0, 0, tiled=True)
    got = got.reshape(n_win, 2, w_dev, r_dev, f_dev)
    offset = lax.axis_index("rcv") * r_dev
    station_ids = offset + jnp.arange(r_dev, dtype=jnp.int32)
    selector = (src_station[:, None] == station_ids[None, :]).astype(jnp.bfloat16)
    rows = jnp.einsum("sr,gcwrf->gcwsf", selector, got, preferred_element_type=jnp.float32)
    src = lax.psum(rows.astype(jnp.bfloat16), "rcv")
    scale = 1.0 / math.sqrt(w_dev * n_win)
    turned = jnp.stack([got[:, 1], -got[:, 0]], axis=1)
    real = jnp.einsum("gcwsf,gcwrf->srf", src, got, preferred_element_type=jnp.float32)
    imag = jnp.einsum("gcwsf,gcwrf->srf", src, turned, preferred_element_type=jnp.float32)
    return jnp.stack([real, imag], axis=2) * scale


def kernel(
    nw, nz, w_dev, r_dev, bins,
    traces, table_hbm, valid_hbm, stations_hbm, out,
    tr, table, spec, snd, got, own, pin, sin, pout, sout, pick, srcf, acc, valid, stations,
    tsem, bsem, isem, ysend, yrecv, psend, precv, ssend, srecv,
):
    me = lax.axis_index("win")
    z = lax.axis_index("rcv")
    f_dev = bins // nw
    n_src = acc.shape[0]
    samples = tr.shape[3]
    half = nw // 2
    units = w_dev // MM
    scale = 1.0 / math.sqrt(w_dev * nw)
    blocks = table.shape[0]
    chip = me // half
    core = lax.rem(me, half)
    near, far = chip * half, (1 - chip) * half
    peers = [far + core, far + (1 - core), near + (1 - core)]
    senders = peers
    barrier = pltpu.get_barrier_semaphore()

    def load(w, h):
        return pltpu.make_async_copy(
            traces.at[w, :, pl.ds(h * samples, samples)], tr.at[w, h], tsem.at[w, h]
        )

    def load_block(b):
        return pltpu.make_async_copy(table_hbm.at[b], table.at[b], bsem.at[b])

    ids = pltpu.make_async_copy(stations_hbm, stations, isem.at[0])
    masks = pltpu.make_async_copy(valid_hbm, valid, isem.at[1])
    ids.start()
    masks.start()
    for h in range(2):
        for w in range(MM):
            load(w, h).start()
        if h == 0:
            load_block(0).start()
    for b in range(1, blocks):
        load_block(b).start()
    for peer in peers:
        pl.semaphore_signal(barrier, inc=1, device_id={"win": peer}, device_id_type=MESH)

    @pl.when(z > 0)
    def _():
        pl.semaphore_signal(barrier, inc=1, device_id={"rcv": z - 1}, device_id_type=MESH)

    @pl.when(z < nz - 1)
    def _():
        pl.semaphore_signal(barrier, inc=1, device_id={"rcv": z + 1}, device_id_type=MESH)

    @pl.when(z == 0)
    def _():
        pin[...] = jnp.zeros_like(pin)

    @pl.when(z == nz - 1)
    def _():
        sin[...] = jnp.zeros_like(sin)

    acc[...] = jnp.zeros_like(acc)
    ids.wait()
    masks.wait()
    here = lax.broadcasted_iota(jnp.int32, (1, r_dev), 1) + z * r_dev
    for s in range(n_src):
        pick[s:s + 1, :] = jnp.where(here == stations[s], 1.0, 0.0).astype(jnp.float32)

    @pl.when((z > 0) & (z < nz - 1))
    def _():
        pl.semaphore_wait(barrier, nw + 1)

    @pl.when((z == 0) | (z == nz - 1))
    def _():
        pl.semaphore_wait(barrier, nw)

    lanes = lax.broadcasted_iota(jnp.int32, (1, BLOCK), 1)
    turn = jnp.where(lax.rem(lanes, 2) == 0, 1.0, -1.0).astype(jnp.float32)

    def y_copy(k, w):
        return pltpu.make_async_remote_copy(
            src_ref=snd.at[peers[k], w], dst_ref=got.at[me, w],
            send_sem=ysend.at[k, w], recv_sem=yrecv.at[k, w],
            device_id={"win": peers[k]}, device_id_type=MESH,
        )

    def y_arrival(k, w):
        return pltpu.make_async_remote_copy(
            src_ref=snd.at[peers[k], w], dst_ref=got.at[senders[k], w],
            send_sem=ysend.at[k, w], recv_sem=yrecv.at[k, w],
            device_id={"win": peers[k]}, device_id_type=MESH,
        )

    def transform(t):
        for wl in range(MM):
            for h in range(2):
                load(t * MM + wl, h).wait()
        x = tr[pl.ds(t * MM, MM)].reshape(MM * 2 * r_dev, samples)
        power = [jnp.zeros((r_dev, 128), jnp.float32) for _ in range(MM)]
        for b in range(blocks):
            @pl.when(t == 0)
            def _(b=b):
                load_block(b).wait()

            both = jnp.dot(x, table[b], preferred_element_type=jnp.float32)
            both = both.reshape(MM, 2, r_dev, BLOCK)
            for wl in range(MM):
                s = both[wl, 0] + turn * both[wl, 1]
                spec[wl, :, b * BLOCK:(b + 1) * BLOCK] = s
                for lo in range(0, BLOCK, 128):
                    part = s[:, lo:lo + 128]
                    power[wl] = power[wl] + part * part

        @pl.when(t == 0)
        def _():
            for w in range(MM, w_dev):
                for h in range(2):
                    load(w, h).start()

        for wl in range(MM):
            w = t * MM + wl
            total = jnp.sum(power[wl], axis=1, keepdims=True) / bins
            gain = lax.rsqrt(total + 1e-06) * valid[w].astype(jnp.float32)
            for d in range(nw):
                for c in range(2):
                    lo = c * bins + d * f_dev
                    snd[d, w, c] = (spec[wl, :, lo:lo + f_dev] * gain).astype(jnp.bfloat16)
            for k in range(nw - 1):
                y_copy(k, w).start()
            got[me, w] = snd[me, w]

    def unit(h, j):
        return (0, pl.ds(j * MM, MM)) if h == 0 else (1, pl.ds(j, 1))

    def sem(h, j):
        return j if h == 0 else units + j

    def right(h, j):
        return pltpu.make_async_remote_copy(
            src_ref=pout.at[unit(h, j)], dst_ref=pin.at[unit(h, j)],
            send_sem=psend.at[sem(h, j)], recv_sem=precv.at[sem(h, j)],
            device_id={"rcv": lax.rem(z + 1, nz)}, device_id_type=MESH,
        )

    def left(h, j):
        return pltpu.make_async_remote_copy(
            src_ref=sout.at[unit(h, j)], dst_ref=sin.at[unit(h, j)],
            send_sem=ssend.at[sem(h, j)], recv_sem=srecv.at[sem(h, j)],
            device_id={"rcv": lax.rem(z + nz - 1, nz)}, device_id_type=MESH,
        )

    def select(h, w):
        rows = pick[...].astype(jnp.bfloat16)
        for gl in range(half):
            for c in range(2):
                own[h, w, gl, c] = jnp.dot(
                    rows, got[(near, far)[h] + gl, w, c], preferred_element_type=jnp.float32
                ).astype(jnp.bfloat16)

    def hops(h, clock, count):
        jr = clock - HOP[h] * z
        jl = clock - HOP[h] * (nz - 1 - z)

        @pl.when((jr >= 0) & (jr < count))
        def _():
            @pl.when(z > 0)
            def _():
                right(h, jr).wait_recv()

            @pl.when(z < nz - 1)
            def _():
                pout[unit(h, jr)] = own[unit(h, jr)] + pin[unit(h, jr)]
                right(h, jr).start()

        @pl.when((jl >= 0) & (jl < count))
        def _():
            @pl.when(z < nz - 1)
            def _():
                left(h, jl).wait_recv()

            @pl.when(z > 0)
            def _():
                sout[unit(h, jl)] = own[unit(h, jl)] + sin[unit(h, jl)]
                left(h, jl).start()

    def correlate(h, first, count, last=False):
        windows = [(gl, wl) for wl in range(count) for gl in range(half)]
        for i, (gl, wl) in enumerate(windows):
            w = first + wl
            for c in range(2):
                srcf[i, c] = (
                    own[h, w, gl, c] + pin[h, w, gl, c] + sin[h, w, gl, c]
                ).astype(jnp.float32)

        def accumulate(q, _):
            sources = []
            for u in range(PAIR):
                sources.append([
                    [
                        jnp.broadcast_to(
                            srcf[i, c, pl.ds(q * PAIR + u, 1), :], (16, f_dev)
                        ).astype(jnp.bfloat16)
                        for c in range(2)
                    ]
                    for i in range(len(windows))
                ])
            for lo in range(0, r_dev, 16):
                rows = slice(lo, lo + 16)
                others = [
                    [got[(near, far)[h] + gl, first + wl, c, rows, :] for c in range(2)]
                    for gl, wl in windows
                ]
                for u in range(PAIR):
                    real, imag = [], []
                    for (sr, si), (rr, ri) in zip(sources[u], others):
                        real.append(sr * rr + si * ri)
                        imag.append(sr * ri - si * rr)
                    while len(real) > 1:
                        real = [a + b for a, b in zip(real[::2], real[1::2])]
                        imag = [a + b for a, b in zip(imag[::2], imag[1::2])]
                    for c, term in enumerate((real[0], imag[0])):
                        total = acc[q * PAIR + u, c, rows, :] + term.astype(jnp.float32)
                        if last:
                            out[q * PAIR + u, pl.ds(2 * lo + c, 16, stride=2), :] = total * scale
                        else:
                            acc[q * PAIR + u, c, rows, :] = total
            return 0

        lax.fori_loop(0, n_src // PAIR, accumulate, 0)

    def step(it, _):
        @pl.when(it < units)
        def _():
            transform(it)
            for wl in range(MM):
                y_arrival(2, it * MM + wl).wait_recv()
                select(0, it * MM + wl)

        hops(0, it, units)

        @pl.when((it >= LAG) & (it < w_dev + LAG))
        def _():
            y_arrival(0, it - LAG).wait_recv()
            y_arrival(1, it - LAG).wait_recv()
            select(1, it - LAG)

        hops(1, it - LAG, w_dev)

        near_unit = it - HOP[0] * (nz - 1)

        @pl.when((near_unit >= 0) & (near_unit < units))
        def _():
            correlate(0, near_unit * MM, MM)

        far_window = it - LAG - HOP[1] * (nz - 1)

        @pl.when((far_window >= 0) & (far_window < w_dev - 1))
        def _():
            correlate(1, far_window, 1)

        @pl.when(far_window == w_dev - 1)
        def _():
            correlate(1, w_dev - 1, 1, True)

        return 0

    lax.fori_loop(0, w_dev + LAG + HOP[1] * (nz - 1), step, 0)

    def drain(w, _):
        for k in range(nw - 1):
            y_copy(k, w).wait_send()
        return 0

    lax.fori_loop(0, w_dev, drain, 0)

    for h, count in ((0, units), (1, w_dev)):
        def drain_chain(j, _, h=h):
            @pl.when(z < nz - 1)
            def _():
                right(h, j).wait_send()

            @pl.when(z > 0)
            def _():
                left(h, j).wait_send()

            return 0

        lax.fori_loop(0, count, drain_chain, 0)


def body(traces, valid, src_station):
    w_dev, r_dev, samples = traces.shape
    nw, nz = lax.axis_size("win"), lax.axis_size("rcv")
    f_dev = F // nw
    n_src = src_station.shape[0]
    if nw != 4 or f_dev % 128 or r_dev % 16 or w_dev % MM or n_src % 4 or samples % 2:
        return plain_body(traces, valid, src_station)
    table = jnp.asarray(half_table(samples, F, samples // 16))
    vmem = pl.BlockSpec(memory_space=pltpu.VMEM)
    bf16, f32 = jnp.bfloat16, jnp.float32
    spectra = (nw, w_dev, 2, r_dev, f_dev)
    rows = (2, w_dev, nw // 2, 2, n_src, f_dev)
    chain = (w_dev // MM + w_dev,)
    hbm = pl.BlockSpec(memory_space=pltpu.HBM)
    dma = pltpu.SemaphoreType.DMA
    stacks = pl.pallas_call(
        functools.partial(kernel, nw, nz, w_dev, r_dev, F),
        out_shape=jax.ShapeDtypeStruct((n_src, 2 * r_dev, f_dev), f32),
        in_specs=[hbm] * 4,
        out_specs=vmem,
        scratch_shapes=[
            pltpu.VMEM((w_dev, 2, r_dev, samples // 2), bf16),
            pltpu.VMEM(table.shape, bf16),
            pltpu.VMEM((MM, r_dev, 2 * F), f32),
            pltpu.VMEM(spectra, bf16),
            pltpu.VMEM(spectra, bf16),
        ] + [pltpu.VMEM(rows, bf16)] * 5 + [
            pltpu.VMEM((n_src, r_dev), f32),
            pltpu.VMEM((MM * nw // 2, 2, n_src, f_dev), f32),
            pltpu.VMEM((n_src, 2, r_dev, f_dev), f32),
            pltpu.SMEM(valid.shape, jnp.int32), pltpu.SMEM(src_station.shape, jnp.int32),
            dma((w_dev, 2)), dma((table.shape[0],)), dma((2,)), dma((nw - 1, w_dev)), dma((nw - 1, w_dev)),
            dma(chain), dma(chain), dma(chain), dma(chain),
        ],
        compiler_params=pltpu.CompilerParams(
            collective_id=0, has_side_effects=True, vmem_limit_bytes=GRANT * 1024 * 1024
        ),
    )(traces, table, valid, src_station)
    return stacks.reshape(n_src, r_dev, 2, f_dev)


def solution(mesh):
    return jax.shard_map(
        body,
        mesh=mesh,
        in_specs=(P("win", ("groups", "rcv"), None), P(("groups", "win")), P("groups")),
        out_specs=P(None, ("groups", "rcv"), None, "win"),
        check_vma=False,
    )
```

```python
import functools
import math

import jax
import jax.numpy as jnp
import ml_dtypes
import numpy as np
from jax import lax
from jax.experimental import pallas as pl
from jax.experimental.pallas import tpu as pltpu
from jax.sharding import PartitionSpec as P

F = 512
BLOCK = 256
MM = 2
GRANT = 48
PAIR = 2
MESH = pl.DeviceIdType.MESH


def band_table(count, bins, first):
    samples = np.arange(count, dtype=np.int64)
    freqs = first + np.arange(bins, dtype=np.int64)
    phase = samples[:, None] * freqs[None, :] % count
    angle = phase.astype(np.float64) * (2.0 * math.pi / count)
    return np.concatenate([np.cos(angle), -np.sin(angle)], axis=1).astype(ml_dtypes.bfloat16)


def half_table(count, bins, first):
    table = band_table(count, bins, first)[: count // 2]
    return np.stack(np.split(table, 2 * bins // BLOCK, axis=1))


def plain_body(traces, valid, src_station):
    w_dev, r_dev, samples = traces.shape
    bins = F
    n_win = lax.axis_size("win")
    f_dev = bins // n_win
    table = jnp.asarray(band_table(samples, bins, samples // 16))
    spectra = jnp.dot(
        traces.reshape(w_dev * r_dev, samples), table, preferred_element_type=jnp.float32
    )
    power = jnp.sum(spectra * spectra, axis=1, keepdims=True) / bins
    keep = jnp.repeat(valid.astype(jnp.float32), r_dev)[:, None]
    white = (spectra * (lax.rsqrt(power + 1e-06) * keep)).astype(jnp.bfloat16)
    white = white.reshape(w_dev * r_dev, 2, n_win, f_dev)
    pieces = jnp.transpose(white, (2, 1, 0, 3))
    got = lax.all_to_all(pieces, "win", 0, 0, tiled=True)
    got = got.reshape(n_win, 2, w_dev, r_dev, f_dev)
    offset = lax.axis_index("rcv") * r_dev
    station_ids = offset + jnp.arange(r_dev, dtype=jnp.int32)
    selector = (src_station[:, None] == station_ids[None, :]).astype(jnp.bfloat16)
    rows = jnp.einsum("sr,gcwrf->gcwsf", selector, got, preferred_element_type=jnp.float32)
    src = lax.psum(rows.astype(jnp.bfloat16), "rcv")
    scale = 1.0 / math.sqrt(w_dev * n_win)
    turned = jnp.stack([got[:, 1], -got[:, 0]], axis=1)
    real = jnp.einsum("gcwsf,gcwrf->srf", src, got, preferred_element_type=jnp.float32)
    imag = jnp.einsum("gcwsf,gcwrf->srf", src, turned, preferred_element_type=jnp.float32)
    return jnp.stack([real, imag], axis=2) * scale


def kernel(
    nw, nz, w_dev, r_dev, bins,
    traces, table_hbm, valid_hbm, stations_hbm, out,
    tr, table, spec, snd, got, own, pin, sin, pout, sout,
    part, part_in, whole, fsrc, pick, srcf, acc, valid, stations,
    tsem, bsem, isem, ysend, yrecv, psend, precv, ssend, srecv,
    rsend, rrecv, qsend, qrecv, gsend, grecv,
):
    me = lax.axis_index("win")
    z = lax.axis_index("rcv")
    f_dev = bins // nw
    n_src = acc.shape[0]
    samples = tr.shape[3]
    half = nw // 2
    units = w_dev // MM
    cuts = nz // 2
    rows_q = n_src // cuts
    scale = 1.0 / math.sqrt(w_dev * nw)
    blocks = table.shape[0]
    chip = me // half
    core = lax.rem(me, half)
    near, far = chip * half, (1 - chip) * half
    peers = [far + core, far + (1 - core), near + (1 - core)]
    barrier = pltpu.get_barrier_semaphore()

    def load(w, h):
        return pltpu.make_async_copy(
            traces.at[w, :, pl.ds(h * samples, samples)], tr.at[w, h], tsem.at[w, h]
        )

    def load_block(b):
        return pltpu.make_async_copy(table_hbm.at[b], table.at[b], bsem.at[b])

    load(0, 0).start()
    load_block(0).start()
    load(0, 1).start()
    for b in range(1, blocks):
        load_block(b).start()
    ids = pltpu.make_async_copy(stations_hbm, stations, isem.at[0])
    masks = pltpu.make_async_copy(valid_hbm, valid, isem.at[1])
    ids.start()
    masks.start()
    for h in range(2):
        load(1, h).start()
    for peer in peers:
        pl.semaphore_signal(barrier, inc=1, device_id={"win": peer}, device_id_type=MESH)
    for step in range(1, nz):
        pl.semaphore_signal(
            barrier, inc=1, device_id={"rcv": lax.rem(z + step, nz)}, device_id_type=MESH
        )

    @pl.when(z == 0)
    def _():
        pin[...] = jnp.zeros_like(pin)

    @pl.when(z == nz - 1)
    def _():
        sin[...] = jnp.zeros_like(sin)

    acc[...] = jnp.zeros_like(acc)
    ids.wait()
    masks.wait()
    here = lax.broadcasted_iota(jnp.int32, (1, r_dev), 1) + z * r_dev
    for s in range(n_src):
        pick[s:s + 1, :] = jnp.where(here == stations[s], 1.0, 0.0).astype(jnp.float32)
    pl.semaphore_wait(barrier, nw - 1 + nz - 1)

    lanes = lax.broadcasted_iota(jnp.int32, (1, BLOCK), 1)
    turn = jnp.where(lax.rem(lanes, 2) == 0, 1.0, -1.0).astype(jnp.float32)

    def y_copy(k, w):
        return pltpu.make_async_remote_copy(
            src_ref=snd.at[peers[k], w], dst_ref=got.at[me, w],
            send_sem=ysend.at[k, w], recv_sem=yrecv.at[k, w],
            device_id={"win": peers[k]}, device_id_type=MESH,
        )

    def y_arrival(k, w):
        return pltpu.make_async_remote_copy(
            src_ref=snd.at[peers[k], w], dst_ref=got.at[peers[k], w],
            send_sem=ysend.at[k, w], recv_sem=yrecv.at[k, w],
            device_id={"win": peers[k]}, device_id_type=MESH,
        )

    def transform(first, count, fresh=False):
        x = tr[pl.ds(first, count)].reshape(count * 2 * r_dev, samples)
        power = [jnp.zeros((r_dev, 128), jnp.float32) for _ in range(count)]
        for b in range(blocks):
            if fresh:
                load_block(b).wait()
            both = jnp.dot(x, table[b], preferred_element_type=jnp.float32)
            both = both.reshape(count, 2, r_dev, BLOCK)
            for wl in range(count):
                s = both[wl, 0] + turn * both[wl, 1]
                spec[wl, :, b * BLOCK:(b + 1) * BLOCK] = s
                for lo in range(0, BLOCK, 128):
                    piece = s[:, lo:lo + 128]
                    power[wl] = power[wl] + piece * piece
        for wl in range(count):
            w = first + wl
            total = jnp.sum(power[wl], axis=1, keepdims=True) / bins
            gain = lax.rsqrt(total + 1e-06) * valid[w].astype(jnp.float32)
            for d in range(nw):
                for c in range(2):
                    lo = c * bins + d * f_dev
                    snd[d, w, c] = (spec[wl, :, lo:lo + f_dev] * gain).astype(jnp.bfloat16)
            y_copy(2, w).start()
            got[me, w] = snd[me, w]

    def bulk(w):
        for k in range(half):
            y_copy(k, w).start()

    def pair(u):
        return pl.ds(u * MM, MM)

    def quarter(q):
        return q // cuts, pl.ds(pl.multiple_of(lax.rem(q, cuts) * rows_q, rows_q), rows_q)

    def spread(step, u):
        c, rows = quarter(lax.rem(z + step, nz))
        return pltpu.make_async_remote_copy(
            src_ref=part.at[:, c, pair(u), rows], dst_ref=part_in.at[step - 1, :, pair(u)],
            send_sem=rsend.at[step - 1, u], recv_sem=rrecv.at[step - 1, u],
            device_id={"rcv": lax.rem(z + step, nz)}, device_id_type=MESH,
        )

    def cross(k, u):
        return pltpu.make_async_remote_copy(
            src_ref=whole.at[peers[k] - far, pair(u)], dst_ref=fsrc.at[core, z, pair(u)],
            send_sem=qsend.at[k, u], recv_sem=qrecv.at[k, u],
            device_id={"win": peers[k]}, device_id_type=MESH,
        )

    def cross_arrival(k, u):
        return pltpu.make_async_remote_copy(
            src_ref=whole.at[peers[k] - far, pair(u)],
            dst_ref=fsrc.at[peers[k] - far, z, pair(u)],
            send_sem=qsend.at[k, u], recv_sem=qrecv.at[k, u],
            device_id={"win": peers[k]}, device_id_type=MESH,
        )

    def share(step, u):
        return pltpu.make_async_remote_copy(
            src_ref=fsrc.at[:, z, pair(u)], dst_ref=fsrc.at[:, z, pair(u)],
            send_sem=gsend.at[step - 1, u], recv_sem=grecv.at[step - 1, u],
            device_id={"rcv": lax.rem(z + step, nz)}, device_id_type=MESH,
        )

    def share_arrival(step, u):
        origin = lax.rem(z + nz - step, nz)
        return pltpu.make_async_remote_copy(
            src_ref=fsrc.at[:, z, pair(u)], dst_ref=fsrc.at[:, origin, pair(u)],
            send_sem=gsend.at[step - 1, u], recv_sem=grecv.at[step - 1, u],
            device_id={"rcv": lax.rem(z + step, nz)}, device_id_type=MESH,
        )

    def select(u):
        rows = pick[...].astype(jnp.bfloat16)
        for wl in range(MM):
            w = u * MM + wl
            for d in range(half):
                for c in range(2):
                    part[d, c, w] = jnp.dot(
                        rows, snd[far + d, w, c], preferred_element_type=jnp.float32
                    ).astype(jnp.bfloat16)
        for step in range(1, nz):
            spread(step, u).start()
        for wl in range(MM):
            w = u * MM + wl
            y_arrival(2, w).wait_recv()
            for gl in range(half):
                for c in range(2):
                    own[w, gl, c] = jnp.dot(
                        rows, got[near + gl, w, c], preferred_element_type=jnp.float32
                    ).astype(jnp.bfloat16)

    def right(u):
        return pltpu.make_async_remote_copy(
            src_ref=pout.at[pair(u)], dst_ref=pin.at[pair(u)],
            send_sem=psend.at[u], recv_sem=precv.at[u],
            device_id={"rcv": lax.rem(z + 1, nz)}, device_id_type=MESH,
        )

    def left(u):
        return pltpu.make_async_remote_copy(
            src_ref=sout.at[pair(u)], dst_ref=sin.at[pair(u)],
            send_sem=ssend.at[u], recv_sem=srecv.at[u],
            device_id={"rcv": lax.rem(z + nz - 1, nz)}, device_id_type=MESH,
        )

    def hops(clock):
        ur = clock - z
        ul = clock - (nz - 1 - z)

        @pl.when((ur >= 0) & (ur < units))
        def _():
            @pl.when(z > 0)
            def _():
                right(ur).wait_recv()

            @pl.when(z < nz - 1)
            def _():
                pout[pair(ur)] = own[pair(ur)] + pin[pair(ur)]
                right(ur).start()

        @pl.when((ul >= 0) & (ul < units))
        def _():
            @pl.when(z < nz - 1)
            def _():
                left(ul).wait_recv()

            @pl.when(z > 0)
            def _():
                sout[pair(ul)] = own[pair(ul)] + sin[pair(ul)]
                left(ul).start()

    def gather_parts(u):
        c, rows = quarter(z)
        for step in range(1, nz):
            spread(step, u).wait_recv()
        total = part[:, c, pair(u), rows]
        for step in range(1, nz):
            total = total + part_in[step - 1, :, pair(u)]
        whole[:, pair(u)] = total
        for k in range(half):
            cross(k, u).start()

    def pass_on(u):
        for k in range(half):
            cross_arrival(k, u).wait_recv()
        for step in range(1, nz):
            share(step, u).start()

    def tick(clock):
        @pl.when((clock >= 1) & (clock <= units))
        def _():
            gather_parts(clock - 1)

        @pl.when((clock >= 1) & (clock + 2 < w_dev))
        def _():
            bulk(clock + 2)

        hops(clock)

        @pl.when((clock >= nz - 1) & (clock < nz - 1 + units))
        def _():
            pass_on(clock - (nz - 1))

    def near_sources(first, count):
        for wl in range(count):
            w = first + wl
            for gl in range(half):
                for c in range(2):
                    srcf[wl * half + gl, c] = (
                        own[w, gl, c] + pin[w, gl, c] + sin[w, gl, c]
                    ).astype(jnp.float32)

    def far_sources(first, count):
        for wl in range(count):
            for gl in range(half):
                for q in range(nz):
                    lo = q % cuts * rows_q
                    srcf[wl * half + gl, q // cuts, lo:lo + rows_q] = (
                        fsrc[gl, q, first + wl].astype(jnp.float32)
                    )

    def correlate(base, first, count, last=False):
        windows = [(gl, wl) for wl in range(count) for gl in range(half)]

        def accumulate(q, _):
            sources = []
            for u in range(PAIR):
                sources.append([
                    [
                        jnp.broadcast_to(
                            srcf[i, c, pl.ds(q * PAIR + u, 1), :], (16, f_dev)
                        ).astype(jnp.bfloat16)
                        for c in range(2)
                    ]
                    for i in range(len(windows))
                ])
            for lo in range(0, r_dev, 16):
                rows = slice(lo, lo + 16)
                others = [
                    [got[base + gl, first + wl, c, rows, :] for c in range(2)]
                    for gl, wl in windows
                ]
                for u in range(PAIR):
                    real, imag = [], []
                    for (sr, si), (rr, ri) in zip(sources[u], others):
                        real.append(sr * rr + si * ri)
                        imag.append(sr * ri - si * rr)
                    while len(real) > 1:
                        real = [a + b for a, b in zip(real[::2], real[1::2])]
                        imag = [a + b for a, b in zip(imag[::2], imag[1::2])]
                    for c, term in enumerate((real[0], imag[0])):
                        total = acc[q * PAIR + u, c, rows, :] + term.astype(jnp.float32)
                        if last:
                            out[q * PAIR + u, pl.ds(2 * lo + c, 16, stride=2), :] = total * scale
                        else:
                            acc[q * PAIR + u, c, rows, :] = total
            return 0

        lax.fori_loop(0, n_src // PAIR, accumulate, 0)

    def build(t, _):
        @pl.when(t == 0)
        def _():
            for wl in range(MM):
                for h in range(2):
                    load(wl, h).wait()
                transform(wl, 1, wl == 0)
                bulk(wl)
                if wl == 0:
                    for w in range(MM, w_dev):
                        for h in range(2):
                            load(w, h).start()

        @pl.when(t > 0)
        def _():
            for wl in range(MM):
                for h in range(2):
                    load(t * MM + wl, h).wait()
            transform(t * MM, MM)

        @pl.when(t == 1)
        def _():
            bulk(MM)

        select(t)
        tick(t)
        return 0

    lax.fori_loop(0, units, build, 0)

    def item(i, _):
        u = i // 2

        @pl.when(lax.rem(i, 2) == 0)
        def _():
            near_sources(u * MM, MM)

        @pl.when(lax.rem(i, 2) == 1)
        def _():
            for step in range(1, nz):
                share_arrival(step, u).wait_recv()
            for wl in range(MM):
                for k in range(half):
                    y_arrival(k, u * MM + wl).wait_recv()
            far_sources(u * MM, MM)

        correlate(near + lax.rem(i, 2) * (far - near), u * MM, MM)

        @pl.when((lax.rem(i, 2) == 0) & (u < nz - 1))
        def _():
            tick(units + u)

        return 0

    lax.fori_loop(0, 2 * units - 1, item, 0)
    for step in range(1, nz):
        share_arrival(step, units - 1).wait_recv()
    for w in range(w_dev - MM, w_dev):
        for k in range(half):
            y_arrival(k, w).wait_recv()
        far_sources(w, 1)
        correlate(far, w, 1, w == w_dev - 1)

    def drain(w, _):
        for k in range(nw - 1):
            y_copy(k, w).wait_send()
        return 0

    lax.fori_loop(0, w_dev, drain, 0)

    def drain_units(u, _):
        for step in range(1, nz):
            spread(step, u).wait_send()
            share(step, u).wait_send()
        for k in range(half):
            cross(k, u).wait_send()

        @pl.when(z < nz - 1)
        def _():
            right(u).wait_send()

        @pl.when(z > 0)
        def _():
            left(u).wait_send()

        return 0

    lax.fori_loop(0, units, drain_units, 0)


def body(traces, valid, src_station):
    w_dev, r_dev, samples = traces.shape
    nw, nz = lax.axis_size("win"), lax.axis_size("rcv")
    f_dev = F // nw
    n_src = src_station.shape[0]
    fits = nw == 4 and nz == 4 and w_dev == 8 and f_dev == 128
    if not fits or r_dev % 16 or n_src % 32 or samples % 512:
        return plain_body(traces, valid, src_station)
    table = jnp.asarray(half_table(samples, F, samples // 16))
    bf16, f32 = jnp.bfloat16, jnp.float32
    units, half, cuts = w_dev // MM, nw // 2, nz // 2
    spectra = (nw, w_dev, 2, r_dev, f_dev)
    rows = (w_dev, half, 2, n_src, f_dev)
    piece = (w_dev, n_src // cuts, f_dev)
    hbm = pl.BlockSpec(memory_space=pltpu.HBM)
    dma = pltpu.SemaphoreType.DMA
    stacks = pl.pallas_call(
        functools.partial(kernel, nw, nz, w_dev, r_dev, F),
        out_shape=jax.ShapeDtypeStruct((n_src, 2 * r_dev, f_dev), f32),
        in_specs=[hbm] * 4,
        out_specs=pl.BlockSpec(memory_space=pltpu.VMEM),
        scratch_shapes=[
            pltpu.VMEM((w_dev, 2, r_dev, samples // 2), bf16),
            pltpu.VMEM(table.shape, bf16),
            pltpu.VMEM((MM, r_dev, 2 * F), f32),
            pltpu.VMEM(spectra, bf16),
            pltpu.VMEM(spectra, bf16),
        ] + [pltpu.VMEM(rows, bf16)] * 5 + [
            pltpu.VMEM((half, 2, w_dev, n_src, f_dev), bf16),
            pltpu.VMEM((nz - 1, half) + piece, bf16),
            pltpu.VMEM((half,) + piece, bf16),
            pltpu.VMEM((half, nz) + piece, bf16),
            pltpu.VMEM((n_src, r_dev), f32),
            pltpu.VMEM((MM * half, 2, n_src, f_dev), f32),
            pltpu.VMEM((n_src, 2, r_dev, f_dev), f32),
            pltpu.SMEM(valid.shape, jnp.int32), pltpu.SMEM(src_station.shape, jnp.int32),
            dma((w_dev, 2)), dma((table.shape[0],)), dma((2,)),
            dma((nw - 1, w_dev)), dma((nw - 1, w_dev)),
            dma((units,)), dma((units,)), dma((units,)), dma((units,)),
            dma((nz - 1, units)), dma((nz - 1, units)),
            dma((half, units)), dma((half, units)),
            dma((nz - 1, units)), dma((nz - 1, units)),
        ],
        compiler_params=pltpu.CompilerParams(
            collective_id=0, has_side_effects=True, vmem_limit_bytes=GRANT * 1024 * 1024
        ),
    )(
        traces, table,
        pltpu.with_memory_space_constraint(valid, pltpu.HBM),
        pltpu.with_memory_space_constraint(src_station, pltpu.HBM),
    )
    return stacks.reshape(n_src, r_dev, 2, f_dev)


def solution(mesh):
    return jax.shard_map(
        body,
        mesh=mesh,
        in_specs=(P("win", ("groups", "rcv"), None), P(("groups", "win")), P("groups")),
        out_specs=P(None, ("groups", "rcv"), None, "win"),
        check_vma=False,
    )
```

```python
import functools
import math

import jax
import jax.numpy as jnp
import ml_dtypes
import numpy as np
from jax import lax
from jax.experimental import pallas as pl
from jax.experimental.pallas import tpu as pltpu
from jax.sharding import PartitionSpec as P

F = 512
BLOCK = 256
MM = 2
GRANT = 48
PAIR = 2
MESH = pl.DeviceIdType.MESH


def band_table(count, bins, first):
    samples = np.arange(count, dtype=np.int64)
    freqs = first + np.arange(bins, dtype=np.int64)
    phase = samples[:, None] * freqs[None, :] % count
    angle = phase.astype(np.float64) * (2.0 * math.pi / count)
    return np.concatenate([np.cos(angle), -np.sin(angle)], axis=1).astype(ml_dtypes.bfloat16)


def half_table(count, bins, first):
    table = band_table(count, bins, first)[: count // 2]
    return np.stack(np.split(table, 2 * bins // BLOCK, axis=1))


def plain_body(traces, valid, src_station):
    w_dev, r_dev, samples = traces.shape
    bins = F
    n_win = lax.axis_size("win")
    f_dev = bins // n_win
    table = jnp.asarray(band_table(samples, bins, samples // 16))
    spectra = jnp.dot(
        traces.reshape(w_dev * r_dev, samples), table, preferred_element_type=jnp.float32
    )
    power = jnp.sum(spectra * spectra, axis=1, keepdims=True) / bins
    keep = jnp.repeat(valid.astype(jnp.float32), r_dev)[:, None]
    white = (spectra * (lax.rsqrt(power + 1e-06) * keep)).astype(jnp.bfloat16)
    white = white.reshape(w_dev * r_dev, 2, n_win, f_dev)
    pieces = jnp.transpose(white, (2, 1, 0, 3))
    got = lax.all_to_all(pieces, "win", 0, 0, tiled=True)
    got = got.reshape(n_win, 2, w_dev, r_dev, f_dev)
    offset = lax.axis_index("rcv") * r_dev
    station_ids = offset + jnp.arange(r_dev, dtype=jnp.int32)
    selector = (src_station[:, None] == station_ids[None, :]).astype(jnp.bfloat16)
    rows = jnp.einsum("sr,gcwrf->gcwsf", selector, got, preferred_element_type=jnp.float32)
    src = lax.psum(rows.astype(jnp.bfloat16), "rcv")
    scale = 1.0 / math.sqrt(w_dev * n_win)
    turned = jnp.stack([got[:, 1], -got[:, 0]], axis=1)
    real = jnp.einsum("gcwsf,gcwrf->srf", src, got, preferred_element_type=jnp.float32)
    imag = jnp.einsum("gcwsf,gcwrf->srf", src, turned, preferred_element_type=jnp.float32)
    return jnp.stack([real, imag], axis=2) * scale


def kernel(
    nw, nz, w_dev, r_dev, bins,
    traces, table_hbm, valid_hbm, stations_hbm, out,
    tr, table, spec, snd, got, own, pin, sin, pout, sout,
    part, part_in, whole, fsrc, nsrc, nout, pick, srcf, acc, valid, stations,
    tsem, bsem, isem, ysend, yrecv, nrecv, psend, precv, ssend, srecv,
    rsend, rrecv, qsend, qrecv, gsend, grecv, wsend, wrecv,
):
    me = lax.axis_index("win")
    z = lax.axis_index("rcv")
    f_dev = bins // nw
    n_src = acc.shape[0]
    samples = tr.shape[3]
    half = nw // 2
    units = w_dev // MM
    cuts = nz // 2
    rows_q = n_src // cuts
    scale = 1.0 / math.sqrt(w_dev * nw)
    blocks = table.shape[0]
    chip = me // half
    core = lax.rem(me, half)
    near, far = chip * half, (1 - chip) * half
    peers = [far + core, far + (1 - core), near + (1 - core)]
    barrier = pltpu.get_barrier_semaphore()

    def load(w, h):
        return pltpu.make_async_copy(
            traces.at[w, :, pl.ds(h * samples, samples)], tr.at[w, h], tsem.at[w, h]
        )

    def load_block(b):
        return pltpu.make_async_copy(table_hbm.at[b], table.at[b], bsem.at[b])

    load(0, 0).start()
    load_block(0).start()
    load(0, 1).start()
    for b in range(1, blocks):
        load_block(b).start()
    ids = pltpu.make_async_copy(stations_hbm, stations, isem.at[0])
    masks = pltpu.make_async_copy(valid_hbm, valid, isem.at[1])
    ids.start()
    masks.start()
    for h in range(2):
        load(1, h).start()
    for peer in peers:
        pl.semaphore_signal(barrier, inc=1, device_id={"win": peer}, device_id_type=MESH)
    for step in range(1, nz):
        pl.semaphore_signal(
            barrier, inc=1, device_id={"rcv": lax.rem(z + step, nz)}, device_id_type=MESH
        )

    @pl.when(z == 0)
    def _():
        pin[...] = jnp.zeros_like(pin)

    @pl.when(z == nz - 1)
    def _():
        sin[...] = jnp.zeros_like(sin)

    acc[...] = jnp.zeros_like(acc)
    ids.wait()
    masks.wait()
    here = lax.broadcasted_iota(jnp.int32, (1, r_dev), 1) + z * r_dev
    for s in range(n_src):
        pick[s:s + 1, :] = jnp.where(here == stations[s], 1.0, 0.0).astype(jnp.float32)
    pl.semaphore_wait(barrier, nw - 1 + nz - 1)

    lanes = lax.broadcasted_iota(jnp.int32, (1, BLOCK), 1)
    turn = jnp.where(lax.rem(lanes, 2) == 0, 1.0, -1.0).astype(jnp.float32)

    def settle(ref, sem):
        pltpu.make_async_copy(ref, ref, sem).wait()

    def y_copy(k, w):
        return pltpu.make_async_remote_copy(
            src_ref=snd.at[peers[k], w], dst_ref=got.at[me, w],
            send_sem=ysend.at[0], recv_sem=yrecv.at[w] if k < half else nrecv.at[w // MM],
            device_id={"win": peers[k]}, device_id_type=MESH,
        )

    def transform(first, count, fresh=False):
        x = tr[pl.ds(first, count)].reshape(count * 2 * r_dev, samples)
        power = [jnp.zeros((r_dev, 128), jnp.float32) for _ in range(count)]
        for b in range(blocks):
            if fresh:
                load_block(b).wait()
            both = jnp.dot(x, table[b], preferred_element_type=jnp.float32)
            both = both.reshape(count, 2, r_dev, BLOCK)
            for wl in range(count):
                s = both[wl, 0] + turn * both[wl, 1]
                spec[wl, :, b * BLOCK:(b + 1) * BLOCK] = s
                for lo in range(0, BLOCK, 128):
                    piece = s[:, lo:lo + 128]
                    power[wl] = power[wl] + piece * piece
        for wl in range(count):
            w = first + wl
            total = jnp.sum(power[wl], axis=1, keepdims=True) / bins
            gain = lax.rsqrt(total + 1e-06) * valid[w].astype(jnp.float32)
            for d in range(nw):
                for c in range(2):
                    lo = c * bins + d * f_dev
                    snd[d, w, c] = (spec[wl, :, lo:lo + f_dev] * gain).astype(jnp.bfloat16)
            y_copy(2, w).start()
            got[me, w] = snd[me, w]

    def bulk(w):
        for k in range(half):
            y_copy(k, w).start()

    def pair(u):
        return pl.ds(u * MM, MM)

    def quarter(q):
        return q // cuts, pl.ds(pl.multiple_of(lax.rem(q, cuts) * rows_q, rows_q), rows_q)

    def spread(step, u):
        c, rows = quarter(lax.rem(z + step, nz))
        return pltpu.make_async_remote_copy(
            src_ref=part.at[:, c, pair(u), rows], dst_ref=part_in.at[step - 1, :, pair(u)],
            send_sem=rsend.at[0], recv_sem=rrecv.at[u],
            device_id={"rcv": lax.rem(z + step, nz)}, device_id_type=MESH,
        )

    def cross(k, u):
        return pltpu.make_async_remote_copy(
            src_ref=whole.at[peers[k] - far, pair(u)], dst_ref=fsrc.at[z, core, pair(u)],
            send_sem=qsend.at[0], recv_sem=qrecv.at[u],
            device_id={"win": peers[k]}, device_id_type=MESH,
        )

    def share(step, u):
        return pltpu.make_async_remote_copy(
            src_ref=fsrc.at[z, :, pair(u)], dst_ref=fsrc.at[z, :, pair(u)],
            send_sem=gsend.at[0], recv_sem=grecv.at[step - 1, u],
            device_id={"rcv": lax.rem(z + step, nz)}, device_id_type=MESH,
        )

    def share_arrival(step, u):
        settle(fsrc.at[lax.rem(z + nz - step, nz), :, pair(u)], grecv.at[step - 1, u])

    def swap(u):
        return pltpu.make_async_remote_copy(
            src_ref=nout.at[pair(u)], dst_ref=nsrc.at[core, pair(u)],
            send_sem=wsend.at[0], recv_sem=wrecv.at[u],
            device_id={"win": peers[2]}, device_id_type=MESH,
        )

    def select(u):
        rows = pick[...].astype(jnp.bfloat16)

        def choose(d, w):
            both = jnp.concatenate([snd[d, w, 0], snd[d, w, 1]], axis=1)
            picked = jnp.dot(rows, both, preferred_element_type=jnp.float32)
            return picked.astype(jnp.bfloat16)

        for wl in range(MM):
            w = u * MM + wl
            for d in range(half):
                picked = choose(far + d, w)
                for c in range(2):
                    part[d, c, w] = picked[:, c * f_dev:(c + 1) * f_dev]
        for step in range(1, nz):
            spread(step, u).start()
        for wl in range(MM):
            w = u * MM + wl
            for d in range(half):
                picked = choose(near + d, w)
                for c in range(2):
                    own[w, d, c] = picked[:, c * f_dev:(c + 1) * f_dev]

    def right(u):
        return pltpu.make_async_remote_copy(
            src_ref=pout.at[pair(u)], dst_ref=pin.at[pair(u)],
            send_sem=psend.at[0], recv_sem=precv.at[u],
            device_id={"rcv": lax.rem(z + 1, nz)}, device_id_type=MESH,
        )

    def left(u):
        return pltpu.make_async_remote_copy(
            src_ref=sout.at[pair(u)], dst_ref=sin.at[pair(u)],
            send_sem=ssend.at[0], recv_sem=srecv.at[u],
            device_id={"rcv": lax.rem(z + nz - 1, nz)}, device_id_type=MESH,
        )

    def hops(clock):
        ur = clock - z
        ul = clock - (nz - 1 - z)

        @pl.when((ur >= 0) & (ur < units))
        def _():
            @pl.when(z > 0)
            def _():
                right(ur).wait_recv()

            @pl.when(z < nz - 1)
            def _():
                pout[pair(ur)] = own[pair(ur)] + pin[pair(ur)]
                right(ur).start()

        @pl.when((ul >= 0) & (ul < units))
        def _():
            @pl.when(z < nz - 1)
            def _():
                left(ul).wait_recv()

            @pl.when(z > 0)
            def _():
                sout[pair(ul)] = own[pair(ul)] + sin[pair(ul)]
                left(ul).start()

    def gather_parts(u):
        c, rows = quarter(z)
        settle(part_in.at[:, :, pair(u)], rrecv.at[u])
        total = part[:, c, pair(u), rows]
        for step in range(1, nz):
            total = total + part_in[step - 1, :, pair(u)]
        whole[:, pair(u)] = total
        for k in range(half):
            cross(k, u).start()

    def pass_on(u):
        settle(fsrc.at[z, :, pair(u)], qrecv.at[u])
        for step in range(1, nz):
            share(step, u).start()

    def finish(u):
        for wl in range(MM):
            w = u * MM + wl
            nout[w] = own[w, 1 - core] + pin[w, 1 - core] + sin[w, 1 - core]
        swap(u).start()
        for wl in range(MM):
            w = u * MM + wl
            nsrc[core, w] = own[w, core] + pin[w, core] + sin[w, core]

    def tick(clock):
        @pl.when((clock >= 1) & (clock <= units))
        def _():
            gather_parts(clock - 1)

        @pl.when(clock == 1)
        def _():
            bulk(MM)

        @pl.when((clock >= 1) & (clock + 2 < w_dev))
        def _():
            bulk(clock + 2)

        hops(clock)

        @pl.when((clock >= nz - 1) & (clock < nz - 1 + units))
        def _():
            finish(clock - (nz - 1))

        @pl.when(clock == 2)
        def _():
            pass_on(0)

        @pl.when((clock >= nz) & (clock < nz - 1 + units))
        def _():
            pass_on(clock - (nz - 1))

    def near_sources(u):
        settle(got.at[near + 1 - core, pair(u)], nrecv.at[u])
        settle(nsrc.at[1 - core, pair(u)], wrecv.at[u])
        for wl in range(MM):
            for gl in range(half):
                srcf[wl * half + gl] = nsrc[gl, u * MM + wl].astype(jnp.float32)

    def far_arrival(w):
        settle(got.at[pl.ds(far, half), w], yrecv.at[w])

    def far_sources(first, count):
        for wl in range(count):
            far_arrival(first + wl)
            for gl in range(half):
                for q in range(nz):
                    lo = q % cuts * rows_q
                    srcf[wl * half + gl, q // cuts, lo:lo + rows_q] = (
                        fsrc[q, gl, first + wl].astype(jnp.float32)
                    )

    def correlate(base, first, count, last=False):
        windows = [(gl, wl) for wl in range(count) for gl in range(half)]

        def accumulate(q, _):
            sources = []
            for u in range(PAIR):
                sources.append([
                    [
                        jnp.broadcast_to(
                            srcf[i, c, pl.ds(q * PAIR + u, 1), :], (16, f_dev)
                        ).astype(jnp.bfloat16)
                        for c in range(2)
                    ]
                    for i in range(len(windows))
                ])
            for lo in range(0, r_dev, 16):
                rows = slice(lo, lo + 16)
                others = [
                    [got[base + gl, first + wl, c, rows, :] for c in range(2)]
                    for gl, wl in windows
                ]
                for u in range(PAIR):
                    real, imag = [], []
                    for (sr, si), (rr, ri) in zip(sources[u], others):
                        real.append(sr * rr + si * ri)
                        imag.append(sr * ri - si * rr)
                    while len(real) > 1:
                        real = [a + b for a, b in zip(real[::2], real[1::2])]
                        imag = [a + b for a, b in zip(imag[::2], imag[1::2])]
                    for c, term in enumerate((real[0], imag[0])):
                        total = acc[q * PAIR + u, c, rows, :] + term.astype(jnp.float32)
                        if last:
                            out[q * PAIR + u, pl.ds(2 * lo + c, 16, stride=2), :] = total * scale
                        else:
                            acc[q * PAIR + u, c, rows, :] = total
            return 0

        lax.fori_loop(0, n_src // PAIR, accumulate, 0)

    def build(t, _):
        @pl.when(t == 0)
        def _():
            for wl in range(MM):
                for h in range(2):
                    load(wl, h).wait()
                transform(wl, 1, wl == 0)
                bulk(wl)
                if wl == 0:
                    for w in range(MM, w_dev):
                        for h in range(2):
                            load(w, h).start()

        @pl.when(t > 0)
        def _():
            for wl in range(MM):
                for h in range(2):
                    load(t * MM + wl, h).wait()
            transform(t * MM, MM)

        select(t)
        tick(t)
        return 0

    lax.fori_loop(0, units, build, 0)

    def item(i, _):
        u = i // 2

        @pl.when(lax.rem(i, 2) == 0)
        def _():
            near_sources(u)

        @pl.when(lax.rem(i, 2) == 1)
        def _():
            for step in range(1, nz):
                share_arrival(step, u)
            far_sources(u * MM, MM)

        correlate(near + lax.rem(i, 2) * (far - near), u * MM, MM)

        @pl.when((lax.rem(i, 2) == 0) & (u < nz - 1))
        def _():
            tick(units + u)

        return 0

    lax.fori_loop(0, 2 * units - 1, item, 0)
    for step in range(1, nz):
        share_arrival(step, units - 1)
    for w in range(w_dev - MM, w_dev):
        far_sources(w, 1)
        correlate(far, w, 1, w == w_dev - 1)

    settle(snd.at[pl.ds(0, nw - 1)], ysend.at[0])
    settle(part_in, rsend.at[0])
    settle(whole, qsend.at[0])
    settle(part_in, gsend.at[0])
    settle(nout, wsend.at[0])

    @pl.when(z < nz - 1)
    def _():
        settle(pout, psend.at[0])

    @pl.when(z > 0)
    def _():
        settle(sout, ssend.at[0])


def body(traces, valid, src_station):
    w_dev, r_dev, samples = traces.shape
    nw, nz = lax.axis_size("win"), lax.axis_size("rcv")
    f_dev = F // nw
    n_src = src_station.shape[0]
    fits = nw == 4 and nz == 4 and w_dev == 8 and f_dev == 128
    if not fits or r_dev % 16 or n_src % 32 or samples % 512:
        return plain_body(traces, valid, src_station)
    table = jnp.asarray(half_table(samples, F, samples // 16))
    bf16, f32 = jnp.bfloat16, jnp.float32
    units, half, cuts = w_dev // MM, nw // 2, nz // 2
    spectra = (nw, w_dev, 2, r_dev, f_dev)
    rows = (w_dev, half, 2, n_src, f_dev)
    piece = (w_dev, n_src // cuts, f_dev)
    hbm = pl.BlockSpec(memory_space=pltpu.HBM)
    dma = pltpu.SemaphoreType.DMA
    stacks = pl.pallas_call(
        functools.partial(kernel, nw, nz, w_dev, r_dev, F),
        out_shape=jax.ShapeDtypeStruct((n_src, 2 * r_dev, f_dev), f32),
        in_specs=[hbm] * 4,
        out_specs=pl.BlockSpec(memory_space=pltpu.VMEM),
        scratch_shapes=[
            pltpu.VMEM((w_dev, 2, r_dev, samples // 2), bf16),
            pltpu.VMEM(table.shape, bf16),
            pltpu.VMEM((MM, r_dev, 2 * F), f32),
            pltpu.VMEM(spectra, bf16),
            pltpu.VMEM(spectra, bf16),
        ] + [pltpu.VMEM(rows, bf16)] * 5 + [
            pltpu.VMEM((half, 2, w_dev, n_src, f_dev), bf16),
            pltpu.VMEM((nz - 1, half) + piece, bf16),
            pltpu.VMEM((half,) + piece, bf16),
            pltpu.VMEM((nz, half) + piece, bf16),
            pltpu.VMEM((half, w_dev, 2, n_src, f_dev), bf16),
            pltpu.VMEM((w_dev, 2, n_src, f_dev), bf16),
            pltpu.VMEM((n_src, r_dev), f32),
            pltpu.VMEM((MM * half, 2, n_src, f_dev), f32),
            pltpu.VMEM((n_src, 2, r_dev, f_dev), f32),
            pltpu.SMEM(valid.shape, jnp.int32), pltpu.SMEM(src_station.shape, jnp.int32),
            dma((w_dev, 2)), dma((table.shape[0],)), dma((2,)),
            dma((1,)), dma((w_dev,)), dma((units,)),
            dma((1,)), dma((units,)), dma((1,)), dma((units,)),
            dma((1,)), dma((units,)), dma((1,)), dma((units,)),
            dma((1,)), dma((nz - 1, units)), dma((1,)), dma((units,)),
        ],
        compiler_params=pltpu.CompilerParams(
            collective_id=0, has_side_effects=True, vmem_limit_bytes=GRANT * 1024 * 1024
        ),
    )(
        traces, table,
        pltpu.with_memory_space_constraint(valid, pltpu.HBM),
        pltpu.with_memory_space_constraint(src_station, pltpu.HBM),
    )
    return stacks.reshape(n_src, r_dev, 2, f_dev)


def solution(mesh):
    return jax.shard_map(
        body,
        mesh=mesh,
        in_specs=(P("win", ("groups", "rcv"), None), P(("groups", "win")), P("groups")),
        out_specs=P(None, ("groups", "rcv"), None, "win"),
        check_vma=False,
    )
```

```python
import functools
import math

import jax
import jax.numpy as jnp
import ml_dtypes
import numpy as np
from jax import lax
from jax.experimental import pallas as pl
from jax.experimental.pallas import tpu as pltpu
from jax.sharding import PartitionSpec as P

F = 512
BLOCK = 256
MM = 2
GRANT = 48
PAIR = 2
MESH = pl.DeviceIdType.MESH


def band_table(count, bins, first):
    samples = np.arange(count, dtype=np.int64)
    freqs = first + np.arange(bins, dtype=np.int64)
    phase = samples[:, None] * freqs[None, :] % count
    angle = phase.astype(np.float64) * (2.0 * math.pi / count)
    return np.concatenate([np.cos(angle), -np.sin(angle)], axis=1).astype(ml_dtypes.bfloat16)


def half_table(count, bins, first):
    table = band_table(count, bins, first)[: count // 2]
    return np.stack(np.split(table, 2 * bins // BLOCK, axis=1))


def plain_body(traces, valid, src_station):
    w_dev, r_dev, samples = traces.shape
    bins = F
    n_win = lax.axis_size("win")
    f_dev = bins // n_win
    table = jnp.asarray(band_table(samples, bins, samples // 16))
    spectra = jnp.dot(
        traces.reshape(w_dev * r_dev, samples), table, preferred_element_type=jnp.float32
    )
    power = jnp.sum(spectra * spectra, axis=1, keepdims=True) / bins
    keep = jnp.repeat(valid.astype(jnp.float32), r_dev)[:, None]
    white = (spectra * (lax.rsqrt(power + 1e-06) * keep)).astype(jnp.bfloat16)
    white = white.reshape(w_dev * r_dev, 2, n_win, f_dev)
    pieces = jnp.transpose(white, (2, 1, 0, 3))
    got = lax.all_to_all(pieces, "win", 0, 0, tiled=True)
    got = got.reshape(n_win, 2, w_dev, r_dev, f_dev)
    offset = lax.axis_index("rcv") * r_dev
    station_ids = offset + jnp.arange(r_dev, dtype=jnp.int32)
    selector = (src_station[:, None] == station_ids[None, :]).astype(jnp.bfloat16)
    rows = jnp.einsum("sr,gcwrf->gcwsf", selector, got, preferred_element_type=jnp.float32)
    src = lax.psum(rows.astype(jnp.bfloat16), "rcv")
    scale = 1.0 / math.sqrt(w_dev * n_win)
    turned = jnp.stack([got[:, 1], -got[:, 0]], axis=1)
    real = jnp.einsum("gcwsf,gcwrf->srf", src, got, preferred_element_type=jnp.float32)
    imag = jnp.einsum("gcwsf,gcwrf->srf", src, turned, preferred_element_type=jnp.float32)
    return jnp.stack([real, imag], axis=2) * scale


ITEMS = ["N0", "F0", "N1", "F1", "F2", "N2", "N3", "F3"]
PLAN = {
    "b0": ["hop 0 0"],
    "a1": ["bulk 3"],
    "b1": ["bulk 2", "hop 0 1", "hop 1 0"],
    "b2": ["gather 0", "bulk 4", "hop 1 1", "hop 2 0"],
    "m3": ["hop 0 2"],
    "b3": ["hop 2 1", "gather 1", "hop 3 0", "pass 0", "gather 2", "bulk 7", "bulk 6", "finish 0", "hop 1 2", "gather 3", "pass 1", "hop 3 1", "hop 2 2"],
    "N0": ["pass 2", "bulk 5", "finish 1"],
    "N1": ["hop 3 2", "finish 2", "pass 3"],
    "F2": ["finish 3"],
}


def kernel(
    nw, nz, w_dev, r_dev, bins,
    traces, table_hbm, valid_hbm, stations_hbm, out,
    tr, table, spec, snd, got, own, pin, sin, pout, sout,
    part, part_in, whole, fsrc, nsrc, nout, pick, srcf, acc, valid, stations,
    tsem, bsem, isem, ysend, yrecv, nrecv, psend, precv, ssend, srecv,
    rsend, rrecv, qsend, qrecv, gsend, grecv, wsend, wrecv,
):
    me = lax.axis_index("win")
    z = lax.axis_index("rcv")
    f_dev = bins // nw
    n_src = acc.shape[0]
    samples = tr.shape[3]
    half = nw // 2
    units = w_dev // MM
    cuts = nz // 2
    rows_q = n_src // cuts
    scale = 1.0 / math.sqrt(w_dev * nw)
    blocks = table.shape[0]
    chip = me // half
    core = lax.rem(me, half)
    near, far = chip * half, (1 - chip) * half
    peers = [far + core, far + (1 - core), near + (1 - core)]
    barrier = pltpu.get_barrier_semaphore()

    def load(w, h):
        return pltpu.make_async_copy(
            traces.at[w, :, pl.ds(h * samples, samples)], tr.at[w, h], tsem.at[w, h]
        )

    def load_block(b):
        return pltpu.make_async_copy(table_hbm.at[b], table.at[b], bsem.at[b])

    load(0, 0).start()
    load_block(0).start()
    load(0, 1).start()
    for b in range(1, blocks):
        load_block(b).start()
    ids = pltpu.make_async_copy(stations_hbm, stations, isem.at[0])
    masks = pltpu.make_async_copy(valid_hbm, valid, isem.at[1])
    ids.start()
    masks.start()
    for h in range(2):
        load(1, h).start()
    for peer in peers:
        pl.semaphore_signal(barrier, inc=1, device_id={"win": peer}, device_id_type=MESH)
    for step in range(1, nz):
        pl.semaphore_signal(
            barrier, inc=1, device_id={"rcv": lax.rem(z + step, nz)}, device_id_type=MESH
        )

    @pl.when(z == 0)
    def _():
        pin[...] = jnp.zeros_like(pin)

    @pl.when(z == nz - 1)
    def _():
        sin[...] = jnp.zeros_like(sin)

    acc[...] = jnp.zeros_like(acc)
    ids.wait()
    masks.wait()
    here = lax.broadcasted_iota(jnp.int32, (1, r_dev), 1) + z * r_dev
    for s in range(n_src):
        pick[s:s + 1, :] = jnp.where(here == stations[s], 1.0, 0.0).astype(jnp.float32)
    pl.semaphore_wait(barrier, nw - 1 + nz - 1)

    lanes = lax.broadcasted_iota(jnp.int32, (1, BLOCK), 1)
    turn = jnp.where(lax.rem(lanes, 2) == 0, 1.0, -1.0).astype(jnp.float32)

    def settle(ref, sem):
        pltpu.make_async_copy(ref, ref, sem).wait()

    def y_copy(k, w):
        return pltpu.make_async_remote_copy(
            src_ref=snd.at[peers[k], w], dst_ref=got.at[me, w],
            send_sem=ysend.at[0], recv_sem=yrecv.at[w] if k < half else nrecv.at[w // MM],
            device_id={"win": peers[k]}, device_id_type=MESH,
        )

    def transform(first, count, fresh=False, point=None):
        x = tr[pl.ds(first, count)].reshape(count * 2 * r_dev, samples)
        power = [jnp.zeros((r_dev, 128), jnp.float32) for _ in range(count)]
        for b in range(blocks):
            if fresh:
                load_block(b).wait()
            if b == blocks // 2 and point:
                run(point)
            both = jnp.dot(x, table[b], preferred_element_type=jnp.float32)
            both = both.reshape(count, 2, r_dev, BLOCK)
            for wl in range(count):
                s = both[wl, 0] + turn * both[wl, 1]
                spec[wl, :, b * BLOCK:(b + 1) * BLOCK] = s
                for lo in range(0, BLOCK, 128):
                    piece = s[:, lo:lo + 128]
                    power[wl] = power[wl] + piece * piece
        for wl in range(count):
            w = first + wl
            total = jnp.sum(power[wl], axis=1, keepdims=True) / bins
            gain = lax.rsqrt(total + 1e-06) * valid[w].astype(jnp.float32)
            for d in range(nw):
                for c in range(2):
                    lo = c * bins + d * f_dev
                    snd[d, w, c] = (spec[wl, :, lo:lo + f_dev] * gain).astype(jnp.bfloat16)
            y_copy(2, w).start()
            got[me, w] = snd[me, w]

    def bulk(w):
        for k in range(half):
            y_copy(k, w).start()

    def pair(u):
        return pl.ds(u * MM, MM)

    def quarter(q):
        return q // cuts, pl.ds(pl.multiple_of(lax.rem(q, cuts) * rows_q, rows_q), rows_q)

    def spread(step, u):
        c, rows = quarter(lax.rem(z + step, nz))
        return pltpu.make_async_remote_copy(
            src_ref=part.at[:, c, pair(u), rows], dst_ref=part_in.at[step - 1, :, pair(u)],
            send_sem=rsend.at[0], recv_sem=rrecv.at[u],
            device_id={"rcv": lax.rem(z + step, nz)}, device_id_type=MESH,
        )

    def cross(k, u):
        return pltpu.make_async_remote_copy(
            src_ref=whole.at[peers[k] - far, pair(u)], dst_ref=fsrc.at[z, core, pair(u)],
            send_sem=qsend.at[0], recv_sem=qrecv.at[u],
            device_id={"win": peers[k]}, device_id_type=MESH,
        )

    def share(step, u):
        return pltpu.make_async_remote_copy(
            src_ref=fsrc.at[z, :, pair(u)], dst_ref=fsrc.at[z, :, pair(u)],
            send_sem=gsend.at[0], recv_sem=grecv.at[step - 1, u],
            device_id={"rcv": lax.rem(z + step, nz)}, device_id_type=MESH,
        )

    def share_arrival(step, u):
        settle(fsrc.at[lax.rem(z + nz - step, nz), :, pair(u)], grecv.at[step - 1, u])

    def swap(u):
        return pltpu.make_async_remote_copy(
            src_ref=nout.at[pair(u)], dst_ref=nsrc.at[core, pair(u)],
            send_sem=wsend.at[0], recv_sem=wrecv.at[u],
            device_id={"win": peers[2]}, device_id_type=MESH,
        )

    def select(u):
        rows = pick[...].astype(jnp.bfloat16)

        def choose(d, w):
            both = jnp.concatenate([snd[d, w, 0], snd[d, w, 1]], axis=1)
            picked = jnp.dot(rows, both, preferred_element_type=jnp.float32)
            return picked.astype(jnp.bfloat16)

        for wl in range(MM):
            w = u * MM + wl
            for d in range(half):
                picked = choose(far + d, w)
                for c in range(2):
                    part[d, c, w] = picked[:, c * f_dev:(c + 1) * f_dev]
        for step in range(1, nz):
            spread(step, u).start()
        for wl in range(MM):
            w = u * MM + wl
            for d in range(half):
                picked = choose(near + d, w)
                for c in range(2):
                    own[w, d, c] = picked[:, c * f_dev:(c + 1) * f_dev]

    def right(u):
        return pltpu.make_async_remote_copy(
            src_ref=pout.at[pair(u)], dst_ref=pin.at[pair(u)],
            send_sem=psend.at[0], recv_sem=precv.at[u],
            device_id={"rcv": lax.rem(z + 1, nz)}, device_id_type=MESH,
        )

    def left(u):
        return pltpu.make_async_remote_copy(
            src_ref=sout.at[pair(u)], dst_ref=sin.at[pair(u)],
            send_sem=ssend.at[0], recv_sem=srecv.at[u],
            device_id={"rcv": lax.rem(z + nz - 1, nz)}, device_id_type=MESH,
        )

    def hop(u, i):
        @pl.when(z == i)
        def _():
            if i > 0:
                right(u).wait_recv()
            if i < nz - 1:
                pout[pair(u)] = own[pair(u)] + pin[pair(u)]
                right(u).start()

        @pl.when(z == nz - 1 - i)
        def _():
            if i > 0:
                left(u).wait_recv()
            if i < nz - 1:
                sout[pair(u)] = own[pair(u)] + sin[pair(u)]
                left(u).start()

    def gather_parts(u):
        c, rows = quarter(z)
        settle(part_in.at[:, :, pair(u)], rrecv.at[u])
        total = part[:, c, pair(u), rows]
        for step in range(1, nz):
            total = total + part_in[step - 1, :, pair(u)]
        whole[:, pair(u)] = total
        for k in range(half):
            cross(k, u).start()

    def pass_on(u):
        settle(fsrc.at[z, :, pair(u)], qrecv.at[u])
        for step in range(1, nz):
            share(step, u).start()

    def finish(u):
        hop(u, nz - 1)
        for wl in range(MM):
            w = u * MM + wl
            nout[w] = own[w, 1 - core] + pin[w, 1 - core] + sin[w, 1 - core]
        swap(u).start()
        for wl in range(MM):
            w = u * MM + wl
            nsrc[core, w] = own[w, core] + pin[w, core] + sin[w, core]

    actions = {
        "hop": hop, "gather": gather_parts, "pass": pass_on, "finish": finish, "bulk": bulk,
    }

    def run(point):
        for entry in PLAN.get(point, []):
            name, *numbers = entry.split()
            actions[name](*[int(n) for n in numbers])

    def near_sources(u):
        settle(got.at[near + 1 - core, pair(u)], nrecv.at[u])
        settle(nsrc.at[1 - core, pair(u)], wrecv.at[u])
        for wl in range(MM):
            for gl in range(half):
                srcf[wl * half + gl] = nsrc[gl, u * MM + wl].astype(jnp.float32)

    def far_arrival(w):
        settle(got.at[pl.ds(far, half), w], yrecv.at[w])

    def far_sources(first, count):
        for wl in range(count):
            far_arrival(first + wl)
            for gl in range(half):
                for q in range(nz):
                    lo = q % cuts * rows_q
                    srcf[wl * half + gl, q // cuts, lo:lo + rows_q] = (
                        fsrc[q, gl, first + wl].astype(jnp.float32)
                    )

    def correlate(base, first, count, last=False):
        windows = [(gl, wl) for wl in range(count) for gl in range(half)]

        def accumulate(q, _):
            sources = []
            for u in range(PAIR):
                sources.append([
                    [
                        jnp.broadcast_to(
                            srcf[i, c, pl.ds(q * PAIR + u, 1), :], (16, f_dev)
                        ).astype(jnp.bfloat16)
                        for c in range(2)
                    ]
                    for i in range(len(windows))
                ])
            for lo in range(0, r_dev, 16):
                rows = slice(lo, lo + 16)
                others = [
                    [got[base + gl, first + wl, c, rows, :] for c in range(2)]
                    for gl, wl in windows
                ]
                for u in range(PAIR):
                    real, imag = [], []
                    for (sr, si), (rr, ri) in zip(sources[u], others):
                        real.append(sr * rr + si * ri)
                        imag.append(sr * ri - si * rr)
                    while len(real) > 1:
                        real = [a + b for a, b in zip(real[::2], real[1::2])]
                        imag = [a + b for a, b in zip(imag[::2], imag[1::2])]
                    for c, term in enumerate((real[0], imag[0])):
                        total = acc[q * PAIR + u, c, rows, :] + term.astype(jnp.float32)
                        if last:
                            out[q * PAIR + u, pl.ds(2 * lo + c, 16, stride=2), :] = total * scale
                        else:
                            acc[q * PAIR + u, c, rows, :] = total
            return 0

        lax.fori_loop(0, n_src // PAIR, accumulate, 0)

    for t in range(units):
        for wl in range(MM):
            for h in range(2):
                load(t * MM + wl, h).wait()
            if t == 0:
                transform(wl, 1, wl == 0)
                bulk(wl)
                if wl == 0:
                    for w in range(MM, w_dev):
                        for h in range(2):
                            load(w, h).start()
        if t > 0:
            transform(t * MM, MM, point=f"m{t}")
        run(f"a{t}")
        select(t)
        run(f"b{t}")
    for name in ITEMS:
        u = int(name[1])
        if name[0] == "N":
            near_sources(u)
            correlate(near, u * MM, MM)
        else:
            for step in range(1, nz):
                share_arrival(step, u)
            if u < units - 1:
                far_sources(u * MM, MM)
                correlate(far, u * MM, MM)
            else:
                for w in range(w_dev - MM, w_dev):
                    far_sources(w, 1)
                    correlate(far, w, 1, w == w_dev - 1)
        run(name)

    settle(snd.at[pl.ds(0, nw - 1)], ysend.at[0])
    settle(part_in, rsend.at[0])
    settle(whole, qsend.at[0])
    settle(part_in, gsend.at[0])
    settle(nout, wsend.at[0])

    @pl.when(z < nz - 1)
    def _():
        settle(pout, psend.at[0])

    @pl.when(z > 0)
    def _():
        settle(sout, ssend.at[0])


def body(traces, valid, src_station):
    w_dev, r_dev, samples = traces.shape
    nw, nz = lax.axis_size("win"), lax.axis_size("rcv")
    f_dev = F // nw
    n_src = src_station.shape[0]
    fits = nw == 4 and nz == 4 and w_dev == 8 and f_dev == 128
    if not fits or r_dev % 16 or n_src % 32 or samples % 512:
        return plain_body(traces, valid, src_station)
    table = jnp.asarray(half_table(samples, F, samples // 16))
    bf16, f32 = jnp.bfloat16, jnp.float32
    units, half, cuts = w_dev // MM, nw // 2, nz // 2
    spectra = (nw, w_dev, 2, r_dev, f_dev)
    rows = (w_dev, half, 2, n_src, f_dev)
    piece = (w_dev, n_src // cuts, f_dev)
    hbm = pl.BlockSpec(memory_space=pltpu.HBM)
    dma = pltpu.SemaphoreType.DMA
    stacks = pl.pallas_call(
        functools.partial(kernel, nw, nz, w_dev, r_dev, F),
        out_shape=jax.ShapeDtypeStruct((n_src, 2 * r_dev, f_dev), f32),
        in_specs=[hbm] * 4,
        out_specs=pl.BlockSpec(memory_space=pltpu.VMEM),
        scratch_shapes=[
            pltpu.VMEM((w_dev, 2, r_dev, samples // 2), bf16),
            pltpu.VMEM(table.shape, bf16),
            pltpu.VMEM((MM, r_dev, 2 * F), f32),
            pltpu.VMEM(spectra, bf16),
            pltpu.VMEM(spectra, bf16),
        ] + [pltpu.VMEM(rows, bf16)] * 5 + [
            pltpu.VMEM((half, 2, w_dev, n_src, f_dev), bf16),
            pltpu.VMEM((nz - 1, half) + piece, bf16),
            pltpu.VMEM((half,) + piece, bf16),
            pltpu.VMEM((nz, half) + piece, bf16),
            pltpu.VMEM((half, w_dev, 2, n_src, f_dev), bf16),
            pltpu.VMEM((w_dev, 2, n_src, f_dev), bf16),
            pltpu.VMEM((n_src, r_dev), f32),
            pltpu.VMEM((MM * half, 2, n_src, f_dev), f32),
            pltpu.VMEM((n_src, 2, r_dev, f_dev), f32),
            pltpu.SMEM(valid.shape, jnp.int32), pltpu.SMEM(src_station.shape, jnp.int32),
            dma((w_dev, 2)), dma((table.shape[0],)), dma((2,)),
            dma((1,)), dma((w_dev,)), dma((units,)),
            dma((1,)), dma((units,)), dma((1,)), dma((units,)),
            dma((1,)), dma((units,)), dma((1,)), dma((units,)),
            dma((1,)), dma((nz - 1, units)), dma((1,)), dma((units,)),
        ],
        compiler_params=pltpu.CompilerParams(
            collective_id=0, has_side_effects=True, vmem_limit_bytes=GRANT * 1024 * 1024
        ),
    )(
        traces, table,
        pltpu.with_memory_space_constraint(valid, pltpu.HBM),
        pltpu.with_memory_space_constraint(src_station, pltpu.HBM),
    )
    return stacks.reshape(n_src, r_dev, 2, f_dev)


def solution(mesh):
    return jax.shard_map(
        body,
        mesh=mesh,
        in_specs=(P("win", ("groups", "rcv"), None), P(("groups", "win")), P("groups")),
        out_specs=P(None, ("groups", "rcv"), None, "win"),
        check_vma=False,
    )
```

```python
import functools
import math

import jax
import jax.numpy as jnp
import ml_dtypes
import numpy as np
from jax import lax
from jax.experimental import pallas as pl
from jax.experimental.pallas import tpu as pltpu
from jax.sharding import PartitionSpec as P

F = 512
BLOCK = 256
MM = 2
UNITS = ((0, 1), (1, 2), (3, 2), (5, 2), (7, 1))
GRANT = 48
PAIR = 2
MESH = pl.DeviceIdType.MESH


def band_table(count, bins, first):
    samples = np.arange(count, dtype=np.int64)
    freqs = first + np.arange(bins, dtype=np.int64)
    phase = samples[:, None] * freqs[None, :] % count
    angle = phase.astype(np.float64) * (2.0 * math.pi / count)
    return np.concatenate([np.cos(angle), -np.sin(angle)], axis=1).astype(ml_dtypes.bfloat16)


def quarter_table(count, bins, first):
    table = band_table(count, bins, first)[: count // 4]
    return np.stack(np.split(table, 2 * bins // BLOCK, axis=1))


def plain_body(traces, valid, src_station):
    w_dev, r_dev, samples = traces.shape
    bins = F
    n_win = lax.axis_size("win")
    f_dev = bins // n_win
    table = jnp.asarray(band_table(samples, bins, samples // 16))
    spectra = jnp.dot(
        traces.reshape(w_dev * r_dev, samples), table, preferred_element_type=jnp.float32
    )
    power = jnp.sum(spectra * spectra, axis=1, keepdims=True) / bins
    keep = jnp.repeat(valid.astype(jnp.float32), r_dev)[:, None]
    white = (spectra * (lax.rsqrt(power + 1e-06) * keep)).astype(jnp.bfloat16)
    white = white.reshape(w_dev * r_dev, 2, n_win, f_dev)
    pieces = jnp.transpose(white, (2, 1, 0, 3))
    got = lax.all_to_all(pieces, "win", 0, 0, tiled=True)
    got = got.reshape(n_win, 2, w_dev, r_dev, f_dev)
    offset = lax.axis_index("rcv") * r_dev
    station_ids = offset + jnp.arange(r_dev, dtype=jnp.int32)
    selector = (src_station[:, None] == station_ids[None, :]).astype(jnp.bfloat16)
    rows = jnp.einsum("sr,gcwrf->gcwsf", selector, got, preferred_element_type=jnp.float32)
    src = lax.psum(rows.astype(jnp.bfloat16), "rcv")
    scale = 1.0 / math.sqrt(w_dev * n_win)
    turned = jnp.stack([got[:, 1], -got[:, 0]], axis=1)
    real = jnp.einsum("gcwsf,gcwrf->srf", src, got, preferred_element_type=jnp.float32)
    imag = jnp.einsum("gcwsf,gcwrf->srf", src, turned, preferred_element_type=jnp.float32)
    return jnp.stack([real, imag], axis=2) * scale


ITEMS = ["N0", "F0", "N1", "F1", "N2", "F2", "N4", "F3", "N3", "F4"]
PLAN = {
    "b0": ["hop 0 0"],
    "m1": ["spread 0"],
    "b1": ["hop 1 0"],
    "l2": ["spread 1", "bulk 2", "hop 0 1"],
    "b2": ["spread 2"],
    "l3": ["hop 1 1", "gather 0"],
    "m3": ["hop 2 0", "hop 0 2", "bulk 4"],
    "l4": ["spread 3", "gather 1"],
    "m4": ["bulk 1", "hop 2 1"],
    "n4": ["pass 0", "hop 1 2"],
    "b4": ["hop 4 0", "spread 4", "gather 2", "bulk 3", "hop 3 0", "gather 3", "finish 0", "pass 1", "hop 4 1"],
    "N0": ["finish 1", "hop 2 2", "hop 3 1"],
    "F0": ["bulk 6", "gather 4", "pass 2"],
    "hN1": ["bulk 5", "hop 4 2"],
    "N1": ["finish 2", "pass 3"],
    "F1": ["hop 3 2"],
    "N2": ["finish 4", "bulk 7", "pass 4"],
    "N4": ["finish 3"],
}


def kernel(
    nw, nz, w_dev, r_dev, bins,
    traces, table_hbm, valid_hbm, stations_hbm, out,
    tr, table, spec, snd, got, own, pin, sin, pout, sout,
    part, part_in, whole, fsrc, nsrc, nout, pick, srcf, acc, valid, stations,
    tsem, bsem, isem, ysend, yrecv, nrecv, psend, precv, ssend, srecv,
    rsend, rrecv, qsend, qrecv, gsend, grecv, wsend, wrecv,
):
    me = lax.axis_index("win")
    z = lax.axis_index("rcv")
    f_dev = bins // nw
    n_src = acc.shape[0]
    samples = tr.shape[3]
    half = nw // 2
    units = len(UNITS)
    cuts = nz // 2
    rows_q = n_src // cuts
    scale = 1.0 / math.sqrt(w_dev * nw)
    blocks = table.shape[0]
    chip = me // half
    core = lax.rem(me, half)
    near, far = chip * half, (1 - chip) * half
    peers = [far + core, far + (1 - core), near + (1 - core)]
    barrier = pltpu.get_barrier_semaphore()

    def load(w, h):
        return pltpu.make_async_copy(
            traces.at[w, :, pl.ds(h * samples, samples)], tr.at[w, h], tsem.at[w, h]
        )

    def load_block(b):
        return pltpu.make_async_copy(
            table_hbm.at[b], table.at[b, pl.ds(0, samples // 2)], bsem.at[b]
        )

    order = [b // 2 + b % 2 * (blocks // 2) for b in range(blocks)]
    load(0, 0).start()
    load_block(0).start()
    load(0, 1).start()
    for b in range(1, blocks):
        load_block(order[b]).start()
    ids = pltpu.make_async_copy(stations_hbm, stations, isem.at[0])
    masks = pltpu.make_async_copy(valid_hbm, valid, isem.at[1])
    ids.start()
    masks.start()
    early = sum(UNITS[1])
    for w in range(1, early):
        for h in range(2):
            load(w, h).start()
    for peer in peers:
        pl.semaphore_signal(barrier, inc=1, device_id={"win": peer}, device_id_type=MESH)
    for step in range(1, nz):
        pl.semaphore_signal(
            barrier, inc=1, device_id={"rcv": lax.rem(z + step, nz)}, device_id_type=MESH
        )

    @pl.when(z == 0)
    def _():
        pin[...] = jnp.zeros_like(pin)

    @pl.when(z == nz - 1)
    def _():
        sin[...] = jnp.zeros_like(sin)

    acc[...] = jnp.zeros_like(acc)
    ids.wait()
    masks.wait()
    here = lax.broadcasted_iota(jnp.int32, (1, r_dev), 1) + z * r_dev
    for s in range(n_src):
        pick[s:s + 1, :] = jnp.where(here == stations[s], 1.0, 0.0).astype(jnp.float32)
    pl.semaphore_wait(barrier, nw - 1 + nz - 1)

    lanes = lax.broadcasted_iota(jnp.int32, (1, BLOCK), 1)
    turn = jnp.where(lax.rem(lanes, 2) == 0, 1.0, -1.0).astype(jnp.float32)

    def owner(w):
        return [u for u, (first, _) in enumerate(UNITS) if first <= w][-1]

    def settle(ref, sem):
        pltpu.make_async_copy(ref, ref, sem).wait()

    def y_copy(k, w):
        return pltpu.make_async_remote_copy(
            src_ref=snd.at[peers[k], w], dst_ref=got.at[me, w],
            send_sem=ysend.at[0], recv_sem=yrecv.at[w] if k < half else nrecv.at[owner(w)],
            device_id={"win": peers[k]}, device_id_type=MESH,
        )

    def extend(b):
        load_block(b).wait()
        load_block(b + blocks // 2).wait()
        keep = jnp.where(lax.rem(lanes, 2) == 0, 1.0, 0.0)
        sign = jnp.where(lax.rem(lanes, 4) < 2, 1.0, -1.0)
        even = (keep * sign).astype(jnp.bfloat16)
        odd = ((1.0 - keep) * sign).astype(jnp.bfloat16)
        quarter_rows = samples // 2

        def rows(i, _):
            lo = pl.multiple_of(i * 64, 64)
            c = table[b, pl.ds(lo, 64), :]
            s = table[b + blocks // 2, pl.ds(lo, 64), :]
            table[b, pl.ds(pl.multiple_of(quarter_rows + lo, 64), 64), :] = c * even + s * odd
            table[b + blocks // 2, pl.ds(pl.multiple_of(quarter_rows + lo, 64), 64), :] = s * even - c * odd
            return 0

        lax.fori_loop(0, quarter_rows // 64, rows, 0)

    def transform(first, count, fresh=False, point=None):
        x = tr[pl.ds(first, count)].reshape(count * 2 * r_dev, samples)
        power = [jnp.zeros((r_dev, 128), jnp.float32) for _ in range(count)]
        for i in range(blocks):
            b = order[i]
            if fresh and b < blocks // 2:
                extend(b)
            if i > 0 and point:
                run("lmn"[i - 1] + point)
            both = jnp.dot(x, table[b], preferred_element_type=jnp.float32)
            both = both.reshape(count, 2, r_dev, BLOCK)
            for wl in range(count):
                s = both[wl, 0] + turn * both[wl, 1]
                spec[wl, :, b * BLOCK:(b + 1) * BLOCK] = s
                for lo in range(0, BLOCK, 128):
                    piece = s[:, lo:lo + 128]
                    power[wl] = power[wl] + piece * piece
        for wl in range(count):
            w = first + wl
            total = jnp.sum(power[wl], axis=1, keepdims=True) / bins
            gain = lax.rsqrt(total + 1e-06) * valid[w].astype(jnp.float32)
            for d in range(nw):
                for c in range(2):
                    lo = c * bins + d * f_dev
                    snd[d, w, c] = (spec[wl, :, lo:lo + f_dev] * gain).astype(jnp.bfloat16)
            y_copy(2, w).start()
            got[me, w] = snd[me, w]

    def bulk(w):
        for k in range(half):
            y_copy(k, w).start()

    def pair(u):
        return pl.ds(*UNITS[u])

    def windows(u):
        return range(UNITS[u][0], sum(UNITS[u]))

    def quarter(q):
        return q // cuts, pl.ds(pl.multiple_of(lax.rem(q, cuts) * rows_q, rows_q), rows_q)

    def spread(step, u):
        c, rows = quarter(lax.rem(z + step, nz))
        return pltpu.make_async_remote_copy(
            src_ref=part.at[:, c, pair(u), rows], dst_ref=part_in.at[step - 1, :, pair(u)],
            send_sem=rsend.at[0], recv_sem=rrecv.at[u],
            device_id={"rcv": lax.rem(z + step, nz)}, device_id_type=MESH,
        )

    def cross(k, u):
        return pltpu.make_async_remote_copy(
            src_ref=whole.at[peers[k] - far, pair(u)], dst_ref=fsrc.at[z, core, pair(u)],
            send_sem=qsend.at[0], recv_sem=qrecv.at[u],
            device_id={"win": peers[k]}, device_id_type=MESH,
        )

    def share(step, u):
        return pltpu.make_async_remote_copy(
            src_ref=fsrc.at[z, :, pair(u)], dst_ref=fsrc.at[z, :, pair(u)],
            send_sem=gsend.at[0], recv_sem=grecv.at[step - 1, u],
            device_id={"rcv": lax.rem(z + step, nz)}, device_id_type=MESH,
        )

    def share_arrival(step, u):
        settle(fsrc.at[lax.rem(z + nz - step, nz), :, pair(u)], grecv.at[step - 1, u])

    def swap(u):
        return pltpu.make_async_remote_copy(
            src_ref=nout.at[pair(u)], dst_ref=nsrc.at[core, pair(u)],
            send_sem=wsend.at[0], recv_sem=wrecv.at[u],
            device_id={"win": peers[2]}, device_id_type=MESH,
        )

    def select(u):
        rows = pick[...].astype(jnp.bfloat16)

        def choose(d, w):
            both = jnp.concatenate([snd[d, w, 0], snd[d, w, 1]], axis=1)
            picked = jnp.dot(rows, both, preferred_element_type=jnp.float32)
            return picked.astype(jnp.bfloat16)

        for w in windows(u):
            for d in range(half):
                picked = choose(far + d, w)
                for c in range(2):
                    part[d, c, w] = picked[:, c * f_dev:(c + 1) * f_dev]
        for w in windows(u):
            for d in range(half):
                picked = choose(near + d, w)
                for c in range(2):
                    own[w, d, c] = picked[:, c * f_dev:(c + 1) * f_dev]

    def right(u):
        return pltpu.make_async_remote_copy(
            src_ref=pout.at[pair(u)], dst_ref=pin.at[pair(u)],
            send_sem=psend.at[0], recv_sem=precv.at[u],
            device_id={"rcv": lax.rem(z + 1, nz)}, device_id_type=MESH,
        )

    def left(u):
        return pltpu.make_async_remote_copy(
            src_ref=sout.at[pair(u)], dst_ref=sin.at[pair(u)],
            send_sem=ssend.at[0], recv_sem=srecv.at[u],
            device_id={"rcv": lax.rem(z + nz - 1, nz)}, device_id_type=MESH,
        )

    def hop(u, i):
        @pl.when(z == i)
        def _():
            if i > 0:
                right(u).wait_recv()
            if i < nz - 1:
                pout[pair(u)] = own[pair(u)] + pin[pair(u)]
                right(u).start()

        @pl.when(z == nz - 1 - i)
        def _():
            if i > 0:
                left(u).wait_recv()
            if i < nz - 1:
                sout[pair(u)] = own[pair(u)] + sin[pair(u)]
                left(u).start()

    def gather_parts(u):
        c, rows = quarter(z)
        settle(part_in.at[:, :, pair(u)], rrecv.at[u])
        total = part[:, c, pair(u), rows]
        for step in range(1, nz):
            total = total + part_in[step - 1, :, pair(u)]
        whole[:, pair(u)] = total
        for k in range(half):
            cross(k, u).start()

    def pass_on(u):
        settle(fsrc.at[z, :, pair(u)], qrecv.at[u])
        for step in range(1, nz):
            share(step, u).start()

    def finish(u):
        hop(u, nz - 1)
        for w in windows(u):
            nout[w] = own[w, 1 - core] + pin[w, 1 - core] + sin[w, 1 - core]
        swap(u).start()
        for w in windows(u):
            nsrc[core, w] = own[w, core] + pin[w, core] + sin[w, core]

    def spread_all(u):
        for step in range(1, nz):
            spread(step, u).start()

    actions = {
        "spread": spread_all, "hop": hop, "gather": gather_parts, "pass": pass_on, "finish": finish, "bulk": bulk,
    }

    def run(point):
        for entry in PLAN.get(point, []):
            name, *numbers = entry.split()
            actions[name](*[int(n) for n in numbers])

    def near_sources(u):
        settle(got.at[near + 1 - core, pair(u)], nrecv.at[u])
        settle(nsrc.at[1 - core, pair(u)], wrecv.at[u])
        for wl, w in enumerate(windows(u)):
            for gl in range(half):
                srcf[wl * half + gl] = nsrc[gl, w].astype(jnp.float32)

    def far_arrival(w):
        settle(got.at[pl.ds(far, half), w], yrecv.at[w])

    def far_sources(first, count):
        for wl in range(count):
            far_arrival(first + wl)
            for gl in range(half):
                for q in range(nz):
                    lo = q % cuts * rows_q
                    srcf[wl * half + gl, q // cuts, lo:lo + rows_q] = (
                        fsrc[q, gl, first + wl].astype(jnp.float32)
                    )

    def correlate(base, first, count, last=False, middle=None):
        windows = [(gl, wl) for wl in range(count) for gl in range(half)]

        def accumulate(q, _):
            sources = []
            for u in range(PAIR):
                sources.append([
                    [
                        jnp.broadcast_to(
                            srcf[i, c, pl.ds(q * PAIR + u, 1), :], (16, f_dev)
                        ).astype(jnp.bfloat16)
                        for c in range(2)
                    ]
                    for i in range(len(windows))
                ])
            for lo in range(0, r_dev, 16):
                rows = slice(lo, lo + 16)
                others = [
                    [got[base + gl, first + wl, c, rows, :] for c in range(2)]
                    for gl, wl in windows
                ]
                for u in range(PAIR):
                    real, imag = [], []
                    for (sr, si), (rr, ri) in zip(sources[u], others):
                        real.append(sr * rr + si * ri)
                        imag.append(sr * ri - si * rr)
                    while len(real) > 1:
                        real = [a + b for a, b in zip(real[::2], real[1::2])]
                        imag = [a + b for a, b in zip(imag[::2], imag[1::2])]
                    for c, term in enumerate((real[0], imag[0])):
                        total = acc[q * PAIR + u, c, rows, :] + term.astype(jnp.float32)
                        if last:
                            out[q * PAIR + u, pl.ds(2 * lo + c, 16, stride=2), :] = total * scale
                        else:
                            acc[q * PAIR + u, c, rows, :] = total
            return 0

        steps = n_src // PAIR
        if middle in PLAN:
            lax.fori_loop(0, steps // 2, accumulate, 0)
            run(middle)
            lax.fori_loop(steps // 2, steps, accumulate, 0)
        else:
            lax.fori_loop(0, steps, accumulate, 0)

    for t in range(units):
        for w in windows(t):
            for h in range(2):
                load(w, h).wait()
        transform(*UNITS[t], fresh=t == 0, point=str(t))
        if t == 0:
            bulk(0)
            for w in range(early, w_dev):
                for h in range(2):
                    load(w, h).start()
        run(f"a{t}")
        select(t)
        run(f"b{t}")
    for name in ITEMS:
        u = int(name[1])
        first, count = UNITS[u]
        if name[0] == "N":
            near_sources(u)
            correlate(near, first, count, middle="h" + name)
        else:
            for step in range(1, nz):
                share_arrival(step, u)
            far_sources(first, count)
            correlate(far, first, count, u == units - 1, middle="h" + name)
        run(name)

    settle(snd.at[pl.ds(0, nw - 1)], ysend.at[0])
    settle(part_in, rsend.at[0])
    settle(whole, qsend.at[0])
    settle(part_in, gsend.at[0])
    settle(nout, wsend.at[0])

    @pl.when(z < nz - 1)
    def _():
        settle(pout, psend.at[0])

    @pl.when(z > 0)
    def _():
        settle(sout, ssend.at[0])


def body(traces, valid, src_station):
    w_dev, r_dev, samples = traces.shape
    nw, nz = lax.axis_size("win"), lax.axis_size("rcv")
    f_dev = F // nw
    n_src = src_station.shape[0]
    fits = nw == 4 and nz == 4 and w_dev == 8 and f_dev == 128
    if not fits or r_dev % 16 or n_src % 32 or samples % 512:
        return plain_body(traces, valid, src_station)
    table = jnp.asarray(quarter_table(samples, F, samples // 16))
    bf16, f32 = jnp.bfloat16, jnp.float32
    units, half, cuts = len(UNITS), nw // 2, nz // 2
    spectra = (nw, w_dev, 2, r_dev, f_dev)
    rows = (w_dev, half, 2, n_src, f_dev)
    piece = (w_dev, n_src // cuts, f_dev)
    hbm = pl.BlockSpec(memory_space=pltpu.HBM)
    dma = pltpu.SemaphoreType.DMA
    stacks = pl.pallas_call(
        functools.partial(kernel, nw, nz, w_dev, r_dev, F),
        out_shape=jax.ShapeDtypeStruct((n_src, 2 * r_dev, f_dev), f32),
        in_specs=[hbm] * 4,
        out_specs=pl.BlockSpec(memory_space=pltpu.VMEM),
        scratch_shapes=[
            pltpu.VMEM((w_dev, 2, r_dev, samples // 2), bf16),
            pltpu.VMEM((table.shape[0], samples // 2, BLOCK), bf16),
            pltpu.VMEM((MM, r_dev, 2 * F), f32),
            pltpu.VMEM(spectra, bf16),
            pltpu.VMEM(spectra, bf16),
        ] + [pltpu.VMEM(rows, bf16)] * 5 + [
            pltpu.VMEM((half, 2, w_dev, n_src, f_dev), bf16),
            pltpu.VMEM((nz - 1, half) + piece, bf16),
            pltpu.VMEM((half,) + piece, bf16),
            pltpu.VMEM((nz, half) + piece, bf16),
            pltpu.VMEM((half, w_dev, 2, n_src, f_dev), bf16),
            pltpu.VMEM((w_dev, 2, n_src, f_dev), bf16),
            pltpu.VMEM((n_src, r_dev), f32),
            pltpu.VMEM((MM * half, 2, n_src, f_dev), f32),
            pltpu.VMEM((n_src, 2, r_dev, f_dev), f32),
            pltpu.SMEM(valid.shape, jnp.int32), pltpu.SMEM(src_station.shape, jnp.int32),
            dma((w_dev, 2)), dma((table.shape[0],)), dma((2,)),
            dma((1,)), dma((w_dev,)), dma((units,)),
            dma((1,)), dma((units,)), dma((1,)), dma((units,)),
            dma((1,)), dma((units,)), dma((1,)), dma((units,)),
            dma((1,)), dma((nz - 1, units)), dma((1,)), dma((units,)),
        ],
        compiler_params=pltpu.CompilerParams(
            collective_id=0, has_side_effects=True, vmem_limit_bytes=GRANT * 1024 * 1024
        ),
    )(
        traces,
        pltpu.with_memory_space_constraint(table, pltpu.HBM),
        pltpu.with_memory_space_constraint(valid, pltpu.HBM),
        pltpu.with_memory_space_constraint(src_station, pltpu.HBM),
    )
    return stacks.reshape(n_src, r_dev, 2, f_dev)


def solution(mesh):
    return jax.shard_map(
        body,
        mesh=mesh,
        in_specs=(P("win", ("groups", "rcv"), None), P(("groups", "win")), P("groups")),
        out_specs=P(None, ("groups", "rcv"), None, "win"),
        check_vma=False,
    )
```

```python
import functools
import math

import jax
import jax.numpy as jnp
import ml_dtypes
import numpy as np
from jax import lax
from jax.experimental import pallas as pl
from jax.experimental.pallas import tpu as pltpu
from jax.sharding import PartitionSpec as P

F = 512
BLOCK = 256
MM = 2
UNITS = ((0, 1), (1, 2), (3, 2), (5, 2), (7, 1))
GRANT = 48
PAIR = 2
MESH = pl.DeviceIdType.MESH


def band_table(count, bins, first):
    samples = np.arange(count, dtype=np.int64)
    freqs = first + np.arange(bins, dtype=np.int64)
    phase = samples[:, None] * freqs[None, :] % count
    angle = phase.astype(np.float64) * (2.0 * math.pi / count)
    return np.concatenate([np.cos(angle), -np.sin(angle)], axis=1).astype(ml_dtypes.bfloat16)


def quarter_table(count, bins, first):
    table = band_table(count, bins, first)[: count // 4]
    return np.stack(np.split(table, 2 * bins // BLOCK, axis=1))


def plain_body(traces, valid, src_station):
    w_dev, r_dev, samples = traces.shape
    bins = F
    n_win = lax.axis_size("win")
    f_dev = bins // n_win
    table = jnp.asarray(band_table(samples, bins, samples // 16))
    spectra = jnp.dot(
        traces.reshape(w_dev * r_dev, samples), table, preferred_element_type=jnp.float32
    )
    power = jnp.sum(spectra * spectra, axis=1, keepdims=True) / bins
    keep = jnp.repeat(valid.astype(jnp.float32), r_dev)[:, None]
    white = (spectra * (lax.rsqrt(power + 1e-06) * keep)).astype(jnp.bfloat16)
    white = white.reshape(w_dev * r_dev, 2, n_win, f_dev)
    pieces = jnp.transpose(white, (2, 1, 0, 3))
    got = lax.all_to_all(pieces, "win", 0, 0, tiled=True)
    got = got.reshape(n_win, 2, w_dev, r_dev, f_dev)
    offset = lax.axis_index("rcv") * r_dev
    station_ids = offset + jnp.arange(r_dev, dtype=jnp.int32)
    selector = (src_station[:, None] == station_ids[None, :]).astype(jnp.bfloat16)
    rows = jnp.einsum("sr,gcwrf->gcwsf", selector, got, preferred_element_type=jnp.float32)
    src = lax.psum(rows.astype(jnp.bfloat16), "rcv")
    scale = 1.0 / math.sqrt(w_dev * n_win)
    turned = jnp.stack([got[:, 1], -got[:, 0]], axis=1)
    real = jnp.einsum("gcwsf,gcwrf->srf", src, got, preferred_element_type=jnp.float32)
    imag = jnp.einsum("gcwsf,gcwrf->srf", src, turned, preferred_element_type=jnp.float32)
    return jnp.stack([real, imag], axis=2) * scale


ITEMS = ["N0", "F0", "N1", "F1", "N2", "F2", "N4", "F3", "N3", "F4"]
PLAN = {
    "b0": ["hop 0 0"],
    "m1": ["spread 0"],
    "b1": ["hop 1 0"],
    "l2": ["spread 1", "bulk 2", "hop 0 1"],
    "b2": ["spread 2"],
    "l3": ["hop 1 1", "gather 0"],
    "m3": ["hop 2 0", "hop 0 2", "bulk 4"],
    "l4": ["spread 3", "gather 1"],
    "m4": ["bulk 1", "hop 2 1"],
    "n4": ["pass 0", "hop 1 2"],
    "b4": ["hop 4 0", "spread 4", "gather 2", "bulk 3", "hop 3 0", "gather 3", "finish 0", "pass 1", "hop 4 1"],
    "N0": ["finish 1", "hop 2 2", "hop 3 1"],
    "F0": ["bulk 6", "gather 4", "pass 2"],
    "hN1": ["bulk 5", "hop 4 2"],
    "N1": ["finish 2", "pass 3"],
    "F1": ["hop 3 2"],
    "N2": ["finish 4", "bulk 7", "pass 4"],
    "N4": ["finish 3"],
}


def kernel(
    nw, nz, w_dev, r_dev, bins,
    traces, table_hbm, valid_hbm, stations_hbm, out,
    tr, table, spec, snd, got, own, pin, sin, pout, sout,
    part, part_in, whole, fsrc, nsrc, nout, pick, srcf, acc, valid, stations,
    tsem, bsem, isem, ysend, yrecv, nrecv, psend, precv, ssend, srecv,
    rsend, rrecv, qsend, qrecv, gsend, grecv, wsend, wrecv,
):
    me = lax.axis_index("win")
    z = lax.axis_index("rcv")
    f_dev = bins // nw
    n_src = acc.shape[0]
    samples = tr.shape[3]
    half = nw // 2
    units = len(UNITS)
    cuts = nz // 2
    rows_q = n_src // cuts
    scale = 1.0 / math.sqrt(w_dev * nw)
    blocks = table.shape[0]
    chip = me // half
    core = lax.rem(me, half)
    near, far = chip * half, (1 - chip) * half
    peers = [far + core, far + (1 - core), near + (1 - core)]
    barrier = pltpu.get_barrier_semaphore()

    def load(w, h):
        return pltpu.make_async_copy(
            traces.at[w, :, pl.ds(h * samples, samples)], tr.at[w, h], tsem.at[w, h]
        )

    def load_block(b):
        return pltpu.make_async_copy(
            table_hbm.at[b], table.at[b, pl.ds(0, samples // 2)], bsem.at[b]
        )

    order = [b // 2 + b % 2 * (blocks // 2) for b in range(blocks)]
    load(0, 0).start()
    load_block(0).start()
    load(0, 1).start()
    for b in range(1, blocks):
        load_block(order[b]).start()
    ids = pltpu.make_async_copy(stations_hbm, stations, isem.at[0])
    masks = pltpu.make_async_copy(valid_hbm, valid, isem.at[1])
    ids.start()
    masks.start()
    early = sum(UNITS[1])
    for w in range(1, early):
        for h in range(2):
            load(w, h).start()
    for peer in peers:
        pl.semaphore_signal(barrier, inc=1, device_id={"win": peer}, device_id_type=MESH)
    for step in range(1, nz):
        pl.semaphore_signal(
            barrier, inc=1, device_id={"rcv": lax.rem(z + step, nz)}, device_id_type=MESH
        )

    @pl.when(z == 0)
    def _():
        pin[...] = jnp.zeros_like(pin)

    @pl.when(z == nz - 1)
    def _():
        sin[...] = jnp.zeros_like(sin)

    acc[...] = jnp.zeros_like(acc)
    ids.wait()
    masks.wait()
    here = lax.broadcasted_iota(jnp.int32, (1, r_dev), 1) + z * r_dev
    for s in range(n_src):
        pick[s:s + 1, :] = jnp.where(here == stations[s], 1.0, 0.0).astype(jnp.float32)

    lanes = lax.broadcasted_iota(jnp.int32, (1, BLOCK), 1)
    turn = jnp.where(lax.rem(lanes, 2) == 0, 1.0, -1.0).astype(jnp.float32)

    def owner(w):
        return [u for u, (first, _) in enumerate(UNITS) if first <= w][-1]

    def settle(ref, sem):
        pltpu.make_async_copy(ref, ref, sem).wait()

    def y_copy(k, w):
        return pltpu.make_async_remote_copy(
            src_ref=snd.at[peers[k], w], dst_ref=got.at[me, w],
            send_sem=ysend.at[0], recv_sem=yrecv.at[w] if k < half else nrecv.at[owner(w)],
            device_id={"win": peers[k]}, device_id_type=MESH,
        )

    def extend(b):
        load_block(b).wait()
        load_block(b + blocks // 2).wait()
        keep = jnp.where(lax.rem(lanes, 2) == 0, 1.0, 0.0)
        sign = jnp.where(lax.rem(lanes, 4) < 2, 1.0, -1.0)
        even = (keep * sign).astype(jnp.bfloat16)
        odd = ((1.0 - keep) * sign).astype(jnp.bfloat16)
        quarter_rows = samples // 2

        def rows(i, _):
            lo = pl.multiple_of(i * 64, 64)
            c = table[b, pl.ds(lo, 64), :]
            s = table[b + blocks // 2, pl.ds(lo, 64), :]
            table[b, pl.ds(pl.multiple_of(quarter_rows + lo, 64), 64), :] = c * even + s * odd
            table[b + blocks // 2, pl.ds(pl.multiple_of(quarter_rows + lo, 64), 64), :] = s * even - c * odd
            return 0

        lax.fori_loop(0, quarter_rows // 64, rows, 0)

    def transform(first, count, fresh=False, point=None):
        x = tr[pl.ds(first, count)].reshape(count * 2 * r_dev, samples)
        power = [jnp.zeros((r_dev, 128), jnp.float32) for _ in range(count)]
        for i in range(blocks):
            b = order[i]
            if fresh and b < blocks // 2:
                extend(b)
            if i > 0 and point:
                run("lmn"[i - 1] + point)
            both = jnp.dot(x, table[b], preferred_element_type=jnp.float32)
            both = both.reshape(count, 2, r_dev, BLOCK)
            for wl in range(count):
                s = both[wl, 0] + turn * both[wl, 1]
                spec[wl, :, b * BLOCK:(b + 1) * BLOCK] = s
                for lo in range(0, BLOCK, 128):
                    piece = s[:, lo:lo + 128]
                    power[wl] = power[wl] + piece * piece
        if fresh:
            pl.semaphore_wait(barrier, nw - 1 + nz - 1)
        for wl in range(count):
            w = first + wl
            total = jnp.sum(power[wl], axis=1, keepdims=True) / bins
            gain = lax.rsqrt(total + 1e-06) * valid[w].astype(jnp.float32)
            for d in range(nw):
                for c in range(2):
                    lo = c * bins + d * f_dev
                    snd[d, w, c] = (spec[wl, :, lo:lo + f_dev] * gain).astype(jnp.bfloat16)
            y_copy(2, w).start()
            got[me, w] = snd[me, w]

    def bulk(w):
        for k in range(half):
            y_copy(k, w).start()

    def pair(u):
        return pl.ds(*UNITS[u])

    def windows(u):
        return range(UNITS[u][0], sum(UNITS[u]))

    def quarter(q):
        return q // cuts, pl.ds(pl.multiple_of(lax.rem(q, cuts) * rows_q, rows_q), rows_q)

    def spread(step, u):
        c, rows = quarter(lax.rem(z + step, nz))
        return pltpu.make_async_remote_copy(
            src_ref=part.at[:, c, pair(u), rows], dst_ref=part_in.at[step - 1, :, pair(u)],
            send_sem=rsend.at[0], recv_sem=rrecv.at[u],
            device_id={"rcv": lax.rem(z + step, nz)}, device_id_type=MESH,
        )

    def cross(k, u):
        return pltpu.make_async_remote_copy(
            src_ref=whole.at[peers[k] - far, pair(u)], dst_ref=fsrc.at[z, core, pair(u)],
            send_sem=qsend.at[0], recv_sem=qrecv.at[u],
            device_id={"win": peers[k]}, device_id_type=MESH,
        )

    def share(step, u):
        return pltpu.make_async_remote_copy(
            src_ref=fsrc.at[z, :, pair(u)], dst_ref=fsrc.at[z, :, pair(u)],
            send_sem=gsend.at[0], recv_sem=grecv.at[step - 1, u],
            device_id={"rcv": lax.rem(z + step, nz)}, device_id_type=MESH,
        )

    def share_arrival(step, u):
        settle(fsrc.at[lax.rem(z + nz - step, nz), :, pair(u)], grecv.at[step - 1, u])

    def swap(u):
        return pltpu.make_async_remote_copy(
            src_ref=nout.at[pair(u)], dst_ref=nsrc.at[core, pair(u)],
            send_sem=wsend.at[0], recv_sem=wrecv.at[u],
            device_id={"win": peers[2]}, device_id_type=MESH,
        )

    def select(u):
        rows = pick[...].astype(jnp.bfloat16)

        def choose(d, w):
            both = jnp.concatenate([snd[d, w, 0], snd[d, w, 1]], axis=1)
            picked = jnp.dot(rows, both, preferred_element_type=jnp.float32)
            return picked.astype(jnp.bfloat16)

        for w in windows(u):
            for d in range(half):
                picked = choose(far + d, w)
                for c in range(2):
                    part[d, c, w] = picked[:, c * f_dev:(c + 1) * f_dev]
        for w in windows(u):
            for d in range(half):
                picked = choose(near + d, w)
                for c in range(2):
                    own[w, d, c] = picked[:, c * f_dev:(c + 1) * f_dev]

    def right(u):
        return pltpu.make_async_remote_copy(
            src_ref=pout.at[pair(u)], dst_ref=pin.at[pair(u)],
            send_sem=psend.at[0], recv_sem=precv.at[u],
            device_id={"rcv": lax.rem(z + 1, nz)}, device_id_type=MESH,
        )

    def left(u):
        return pltpu.make_async_remote_copy(
            src_ref=sout.at[pair(u)], dst_ref=sin.at[pair(u)],
            send_sem=ssend.at[0], recv_sem=srecv.at[u],
            device_id={"rcv": lax.rem(z + nz - 1, nz)}, device_id_type=MESH,
        )

    def hop(u, i):
        @pl.when(z == i)
        def _():
            if i > 0:
                right(u).wait_recv()
            if i < nz - 1:
                pout[pair(u)] = own[pair(u)] + pin[pair(u)]
                right(u).start()

        @pl.when(z == nz - 1 - i)
        def _():
            if i > 0:
                left(u).wait_recv()
            if i < nz - 1:
                sout[pair(u)] = own[pair(u)] + sin[pair(u)]
                left(u).start()

    def gather_parts(u):
        c, rows = quarter(z)
        settle(part_in.at[:, :, pair(u)], rrecv.at[u])
        total = part[:, c, pair(u), rows]
        for step in range(1, nz):
            total = total + part_in[step - 1, :, pair(u)]
        whole[:, pair(u)] = total
        for k in range(half):
            cross(k, u).start()

    def pass_on(u):
        settle(fsrc.at[z, :, pair(u)], qrecv.at[u])
        for step in range(1, nz):
            share(step, u).start()

    def finish(u):
        hop(u, nz - 1)
        for w in windows(u):
            nout[w] = own[w, 1 - core] + pin[w, 1 - core] + sin[w, 1 - core]
        swap(u).start()
        for w in windows(u):
            nsrc[core, w] = own[w, core] + pin[w, core] + sin[w, core]

    def spread_all(u):
        for step in range(1, nz):
            spread(step, u).start()

    actions = {
        "spread": spread_all, "hop": hop, "gather": gather_parts, "pass": pass_on, "finish": finish, "bulk": bulk,
    }

    def run(point):
        for entry in PLAN.get(point, []):
            name, *numbers = entry.split()
            actions[name](*[int(n) for n in numbers])

    def near_sources(u):
        settle(got.at[near + 1 - core, pair(u)], nrecv.at[u])
        settle(nsrc.at[1 - core, pair(u)], wrecv.at[u])
        for wl, w in enumerate(windows(u)):
            for gl in range(half):
                srcf[wl * half + gl] = nsrc[gl, w].astype(jnp.float32)

    def far_arrival(w):
        settle(got.at[pl.ds(far, half), w], yrecv.at[w])

    def far_sources(first, count):
        for wl in range(count):
            far_arrival(first + wl)
            for gl in range(half):
                for q in range(nz):
                    lo = q % cuts * rows_q
                    srcf[wl * half + gl, q // cuts, lo:lo + rows_q] = (
                        fsrc[q, gl, first + wl].astype(jnp.float32)
                    )

    def correlate(base, first, count, last=False, middle=None):
        windows = [(gl, wl) for wl in range(count) for gl in range(half)]

        def accumulate(q, _):
            sources = []
            for u in range(PAIR):
                sources.append([
                    [
                        jnp.broadcast_to(
                            srcf[i, c, pl.ds(q * PAIR + u, 1), :], (16, f_dev)
                        ).astype(jnp.bfloat16)
                        for c in range(2)
                    ]
                    for i in range(len(windows))
                ])
            for lo in range(0, r_dev, 16):
                rows = slice(lo, lo + 16)
                others = [
                    [got[base + gl, first + wl, c, rows, :] for c in range(2)]
                    for gl, wl in windows
                ]
                for u in range(PAIR):
                    real, imag = [], []
                    for (sr, si), (rr, ri) in zip(sources[u], others):
                        real.append(sr * rr + si * ri)
                        imag.append(sr * ri - si * rr)
                    while len(real) > 1:
                        real = [a + b for a, b in zip(real[::2], real[1::2])]
                        imag = [a + b for a, b in zip(imag[::2], imag[1::2])]
                    for c, term in enumerate((real[0], imag[0])):
                        total = acc[q * PAIR + u, c, rows, :] + term.astype(jnp.float32)
                        if last:
                            out[q * PAIR + u, pl.ds(2 * lo + c, 16, stride=2), :] = total * scale
                        else:
                            acc[q * PAIR + u, c, rows, :] = total
            return 0

        steps = n_src // PAIR
        if middle in PLAN:
            lax.fori_loop(0, steps // 2, accumulate, 0)
            run(middle)
            lax.fori_loop(steps // 2, steps, accumulate, 0)
        else:
            lax.fori_loop(0, steps, accumulate, 0)

    for t in range(units):
        for w in windows(t):
            for h in range(2):
                load(w, h).wait()
        transform(*UNITS[t], fresh=t == 0, point=str(t))
        if t == 0:
            bulk(0)
            for w in range(early, w_dev):
                for h in range(2):
                    load(w, h).start()
        run(f"a{t}")
        select(t)
        run(f"b{t}")
    for name in ITEMS:
        u = int(name[1])
        first, count = UNITS[u]
        if name[0] == "N":
            near_sources(u)
            correlate(near, first, count, middle="h" + name)
        else:
            for step in range(1, nz):
                share_arrival(step, u)
            far_sources(first, count)
            correlate(far, first, count, u == units - 1, middle="h" + name)
        run(name)

    settle(snd.at[pl.ds(0, nw - 1)], ysend.at[0])
    settle(part_in, rsend.at[0])
    settle(whole, qsend.at[0])
    settle(part_in, gsend.at[0])
    settle(nout, wsend.at[0])

    @pl.when(z < nz - 1)
    def _():
        settle(pout, psend.at[0])

    @pl.when(z > 0)
    def _():
        settle(sout, ssend.at[0])


def body(traces, valid, src_station):
    w_dev, r_dev, samples = traces.shape
    nw, nz = lax.axis_size("win"), lax.axis_size("rcv")
    f_dev = F // nw
    n_src = src_station.shape[0]
    fits = nw == 4 and nz == 4 and w_dev == 8 and f_dev == 128
    if not fits or r_dev % 16 or n_src % 32 or samples % 512:
        return plain_body(traces, valid, src_station)
    table = jnp.asarray(quarter_table(samples, F, samples // 16))
    bf16, f32 = jnp.bfloat16, jnp.float32
    units, half, cuts = len(UNITS), nw // 2, nz // 2
    spectra = (nw, w_dev, 2, r_dev, f_dev)
    rows = (w_dev, half, 2, n_src, f_dev)
    piece = (w_dev, n_src // cuts, f_dev)
    hbm = pl.BlockSpec(memory_space=pltpu.HBM)
    dma = pltpu.SemaphoreType.DMA
    stacks = pl.pallas_call(
        functools.partial(kernel, nw, nz, w_dev, r_dev, F),
        out_shape=jax.ShapeDtypeStruct((n_src, 2 * r_dev, f_dev), f32),
        in_specs=[hbm] * 4,
        out_specs=pl.BlockSpec(memory_space=pltpu.VMEM),
        scratch_shapes=[
            pltpu.VMEM((w_dev, 2, r_dev, samples // 2), bf16),
            pltpu.VMEM((table.shape[0], samples // 2, BLOCK), bf16),
            pltpu.VMEM((MM, r_dev, 2 * F), f32),
            pltpu.VMEM(spectra, bf16),
            pltpu.VMEM(spectra, bf16),
        ] + [pltpu.VMEM(rows, bf16)] * 5 + [
            pltpu.VMEM((half, 2, w_dev, n_src, f_dev), bf16),
            pltpu.VMEM((nz - 1, half) + piece, bf16),
            pltpu.VMEM((half,) + piece, bf16),
            pltpu.VMEM((nz, half) + piece, bf16),
            pltpu.VMEM((half, w_dev, 2, n_src, f_dev), bf16),
            pltpu.VMEM((w_dev, 2, n_src, f_dev), bf16),
            pltpu.VMEM((n_src, r_dev), f32),
            pltpu.VMEM((MM * half, 2, n_src, f_dev), f32),
            pltpu.VMEM((n_src, 2, r_dev, f_dev), f32),
            pltpu.SMEM(valid.shape, jnp.int32), pltpu.SMEM(src_station.shape, jnp.int32),
            dma((w_dev, 2)), dma((table.shape[0],)), dma((2,)),
            dma((1,)), dma((w_dev,)), dma((units,)),
            dma((1,)), dma((units,)), dma((1,)), dma((units,)),
            dma((1,)), dma((units,)), dma((1,)), dma((units,)),
            dma((1,)), dma((nz - 1, units)), dma((1,)), dma((units,)),
        ],
        compiler_params=pltpu.CompilerParams(
            collective_id=0, has_side_effects=True, vmem_limit_bytes=GRANT * 1024 * 1024
        ),
    )(
        traces,
        pltpu.with_memory_space_constraint(table, pltpu.HBM),
        pltpu.with_memory_space_constraint(valid, pltpu.HBM),
        pltpu.with_memory_space_constraint(src_station, pltpu.HBM),
    )
    return stacks.reshape(n_src, r_dev, 2, f_dev)


def solution(mesh):
    return jax.shard_map(
        body,
        mesh=mesh,
        in_specs=(P("win", ("groups", "rcv"), None), P(("groups", "win")), P("groups")),
        out_specs=P(None, ("groups", "rcv"), None, "win"),
        check_vma=False,
    )
```

```python
import functools
import math

import jax
import jax.numpy as jnp
import ml_dtypes
import numpy as np
from jax import lax
from jax.experimental import pallas as pl
from jax.experimental.pallas import tpu as pltpu
from jax.sharding import PartitionSpec as P

F = 512
BLOCK = 256
MM = 2
UNITS = ((0, 1), (1, 2), (3, 2), (5, 2), (7, 1))
GRANT = 48
PAIR = 2
MESH = pl.DeviceIdType.MESH


def band_table(count, bins, first):
    samples = np.arange(count, dtype=np.int64)
    freqs = first + np.arange(bins, dtype=np.int64)
    phase = samples[:, None] * freqs[None, :] % count
    angle = phase.astype(np.float64) * (2.0 * math.pi / count)
    return np.concatenate([np.cos(angle), -np.sin(angle)], axis=1).astype(ml_dtypes.bfloat16)


def quarter_table(count, bins, first):
    table = band_table(count, bins, first)[: count // 4]
    return np.stack(np.split(table, 2 * bins // BLOCK, axis=1))


def plain_body(traces, valid, src_station):
    w_dev, r_dev, samples = traces.shape
    bins = F
    n_win = lax.axis_size("win")
    f_dev = bins // n_win
    table = jnp.asarray(band_table(samples, bins, samples // 16))
    spectra = jnp.dot(
        traces.reshape(w_dev * r_dev, samples), table, preferred_element_type=jnp.float32
    )
    power = jnp.sum(spectra * spectra, axis=1, keepdims=True) / bins
    keep = jnp.repeat(valid.astype(jnp.float32), r_dev)[:, None]
    white = (spectra * (lax.rsqrt(power + 1e-06) * keep)).astype(jnp.bfloat16)
    white = white.reshape(w_dev * r_dev, 2, n_win, f_dev)
    pieces = jnp.transpose(white, (2, 1, 0, 3))
    got = lax.all_to_all(pieces, "win", 0, 0, tiled=True)
    got = got.reshape(n_win, 2, w_dev, r_dev, f_dev)
    offset = lax.axis_index("rcv") * r_dev
    station_ids = offset + jnp.arange(r_dev, dtype=jnp.int32)
    selector = (src_station[:, None] == station_ids[None, :]).astype(jnp.bfloat16)
    rows = jnp.einsum("sr,gcwrf->gcwsf", selector, got, preferred_element_type=jnp.float32)
    src = lax.psum(rows.astype(jnp.bfloat16), "rcv")
    scale = 1.0 / math.sqrt(w_dev * n_win)
    turned = jnp.stack([got[:, 1], -got[:, 0]], axis=1)
    real = jnp.einsum("gcwsf,gcwrf->srf", src, got, preferred_element_type=jnp.float32)
    imag = jnp.einsum("gcwsf,gcwrf->srf", src, turned, preferred_element_type=jnp.float32)
    return jnp.stack([real, imag], axis=2) * scale


ITEMS = ["N0", "F0", "N1", "F1", "N2", "F2", "N4", "F3", "N3", "F4"]
PLAN = {
    "b0": ["hop 0 0"],
    "m1": ["spread 0"],
    "b1": ["hop 1 0"],
    "l2": ["spread 1", "bulk 2", "hop 0 1"],
    "b2": ["spread 2"],
    "l3": ["hop 1 1", "gather 0"],
    "m3": ["hop 2 0", "hop 0 2", "bulk 4"],
    "l4": ["spread 3", "gather 1"],
    "m4": ["bulk 1", "hop 2 1"],
    "n4": ["pass 0", "hop 1 2"],
    "b4": ["hop 4 0", "spread 4", "gather 2", "bulk 3", "hop 3 0", "gather 3", "finish 0", "pass 1", "hop 4 1"],
    "N0": ["finish 1", "hop 2 2", "hop 3 1"],
    "F0": ["bulk 6", "gather 4", "pass 2"],
    "hN1": ["bulk 5", "hop 4 2"],
    "N1": ["finish 2", "pass 3"],
    "F1": ["hop 3 2"],
    "N2": ["finish 4", "bulk 7", "pass 4"],
    "N4": ["finish 3"],
}


def kernel(
    nw, nz, w_dev, r_dev, bins,
    traces, table_hbm, valid_hbm, stations_hbm, out,
    tr, table, spec, snd, got, own, pin, sin, pout, sout,
    part, part_in, whole, fsrc, nsrc, nout, pick, srcf, acc, valid, stations,
    tsem, bsem, isem, ysend, yrecv, nrecv, psend, precv, ssend, srecv,
    rsend, rrecv, qsend, qrecv, gsend, grecv, wsend, wrecv,
):
    me = lax.axis_index("win")
    z = lax.axis_index("rcv")
    f_dev = bins // nw
    n_src = acc.shape[0]
    samples = tr.shape[3]
    half = nw // 2
    units = len(UNITS)
    cuts = nz // 2
    rows_q = n_src // cuts
    scale = 1.0 / math.sqrt(w_dev * nw)
    blocks = table.shape[0]
    chip = me // half
    core = lax.rem(me, half)
    near, far = chip * half, (1 - chip) * half
    peers = [far + core, far + (1 - core), near + (1 - core)]
    barrier = pltpu.get_barrier_semaphore()

    def load(w, h):
        return pltpu.make_async_copy(
            traces.at[w, :, pl.ds(h * samples, samples)], tr.at[w, h], tsem.at[w, h]
        )

    def load_block(b):
        return pltpu.make_async_copy(
            table_hbm.at[b], table.at[b, pl.ds(0, samples // 2)], bsem.at[b]
        )

    order = [b // 2 + b % 2 * (blocks // 2) for b in range(blocks)]
    load(0, 0).start()
    load_block(0).start()
    load(0, 1).start()
    for b in range(1, blocks):
        load_block(order[b]).start()
    ids = pltpu.make_async_copy(stations_hbm, stations, isem.at[0])
    masks = pltpu.make_async_copy(valid_hbm, valid, isem.at[1])
    ids.start()
    masks.start()
    early = sum(UNITS[1])
    for w in range(1, early):
        for h in range(2):
            load(w, h).start()
    for peer in peers:
        pl.semaphore_signal(barrier, inc=1, device_id={"win": peer}, device_id_type=MESH)
    for step in range(1, nz):
        pl.semaphore_signal(
            barrier, inc=1, device_id={"rcv": lax.rem(z + step, nz)}, device_id_type=MESH
        )

    @pl.when(z == 0)
    def _():
        pin[...] = jnp.zeros_like(pin)

    @pl.when(z == nz - 1)
    def _():
        sin[...] = jnp.zeros_like(sin)

    acc[...] = jnp.zeros_like(acc)
    ids.wait()
    masks.wait()
    here = lax.broadcasted_iota(jnp.int32, (1, r_dev), 1) + z * r_dev
    for s in range(n_src):
        pick[s:s + 1, :] = jnp.where(here == stations[s], 1.0, 0.0).astype(jnp.float32)

    lanes = lax.broadcasted_iota(jnp.int32, (1, BLOCK), 1)
    turn = jnp.where(lax.rem(lanes, 2) == 0, 1.0, -1.0).astype(jnp.float32)

    def owner(w):
        return [u for u, (first, _) in enumerate(UNITS) if first <= w][-1]

    def settle(ref, sem):
        pltpu.make_async_copy(ref, ref, sem).wait()

    def y_copy(k, w):
        return pltpu.make_async_remote_copy(
            src_ref=snd.at[peers[k], w], dst_ref=got.at[me, w],
            send_sem=ysend.at[0], recv_sem=yrecv.at[w] if k < half else nrecv.at[owner(w)],
            device_id={"win": peers[k]}, device_id_type=MESH,
        )

    def extend(b):
        load_block(b).wait()
        load_block(b + blocks // 2).wait()
        keep = jnp.where(lax.rem(lanes, 2) == 0, 1.0, 0.0)
        sign = jnp.where(lax.rem(lanes, 4) < 2, 1.0, -1.0)
        even = (keep * sign).astype(jnp.bfloat16)
        odd = ((1.0 - keep) * sign).astype(jnp.bfloat16)
        quarter_rows = samples // 2

        def rows(i, _):
            lo = pl.multiple_of(i * 64, 64)
            c = table[b, pl.ds(lo, 64), :]
            s = table[b + blocks // 2, pl.ds(lo, 64), :]
            table[b, pl.ds(pl.multiple_of(quarter_rows + lo, 64), 64), :] = c * even + s * odd
            table[b + blocks // 2, pl.ds(pl.multiple_of(quarter_rows + lo, 64), 64), :] = s * even - c * odd
            return 0

        lax.fori_loop(0, quarter_rows // 64, rows, 0)

    def transform(first, count, fresh=False, point=None):
        x = tr[pl.ds(first, count)].reshape(count * 2 * r_dev, samples)
        power = [jnp.zeros((r_dev, 128), jnp.float32) for _ in range(count)]
        for i in range(blocks):
            b = order[i]
            if fresh and b < blocks // 2:
                extend(b)
            if i > 0 and point:
                run("lmn"[i - 1] + point)
            both = jnp.dot(x, table[b], preferred_element_type=jnp.float32)
            both = both.reshape(count, 2, r_dev, BLOCK)
            for wl in range(count):
                s = both[wl, 0] + turn * both[wl, 1]
                spec[wl, :, b * BLOCK:(b + 1) * BLOCK] = s
                for lo in range(0, BLOCK, 128):
                    piece = s[:, lo:lo + 128]
                    power[wl] = power[wl] + piece * piece
        if fresh:
            pl.semaphore_wait(barrier, nw - 1 + nz - 1)
        for wl in range(count):
            w = first + wl
            total = jnp.sum(power[wl], axis=1, keepdims=True) / bins
            gain = lax.rsqrt(total + 1e-06) * valid[w].astype(jnp.float32)
            for d in range(nw):
                for c in range(2):
                    lo = c * bins + d * f_dev
                    snd[d, w, c] = (spec[wl, :, lo:lo + f_dev] * gain).astype(jnp.bfloat16)
            y_copy(2, w).start()
            got[me, w] = snd[me, w]

    def bulk(w):
        for k in range(half):
            y_copy(k, w).start()

    def pair(u):
        return pl.ds(*UNITS[u])

    def windows(u):
        return range(UNITS[u][0], sum(UNITS[u]))

    def quarter(q):
        return q // cuts, pl.ds(pl.multiple_of(lax.rem(q, cuts) * rows_q, rows_q), rows_q)

    def spread(step, u):
        c, rows = quarter(lax.rem(z + step, nz))
        return pltpu.make_async_remote_copy(
            src_ref=part.at[:, c, pair(u), rows], dst_ref=part_in.at[step - 1, :, pair(u)],
            send_sem=rsend.at[0], recv_sem=rrecv.at[u],
            device_id={"rcv": lax.rem(z + step, nz)}, device_id_type=MESH,
        )

    def cross(k, u):
        return pltpu.make_async_remote_copy(
            src_ref=whole.at[peers[k] - far, pair(u)], dst_ref=fsrc.at[z, core, pair(u)],
            send_sem=qsend.at[0], recv_sem=qrecv.at[u],
            device_id={"win": peers[k]}, device_id_type=MESH,
        )

    def share(step, u):
        return pltpu.make_async_remote_copy(
            src_ref=fsrc.at[z, :, pair(u)], dst_ref=fsrc.at[z, :, pair(u)],
            send_sem=gsend.at[0], recv_sem=grecv.at[step - 1, u],
            device_id={"rcv": lax.rem(z + step, nz)}, device_id_type=MESH,
        )

    def share_arrival(step, u):
        settle(fsrc.at[lax.rem(z + nz - step, nz), :, pair(u)], grecv.at[step - 1, u])

    def swap(u):
        return pltpu.make_async_remote_copy(
            src_ref=nout.at[pair(u)], dst_ref=nsrc.at[core, pair(u)],
            send_sem=wsend.at[0], recv_sem=wrecv.at[u],
            device_id={"win": peers[2]}, device_id_type=MESH,
        )

    def select(u):
        rows = pick[...].astype(jnp.bfloat16)

        def choose(d, w):
            both = jnp.concatenate([snd[d, w, 0], snd[d, w, 1]], axis=1)
            picked = jnp.dot(rows, both, preferred_element_type=jnp.float32)
            return picked.astype(jnp.bfloat16)

        for w in windows(u):
            for d in range(half):
                picked = choose(far + d, w)
                for c in range(2):
                    part[d, c, w] = picked[:, c * f_dev:(c + 1) * f_dev]
        for w in windows(u):
            for d in range(half):
                picked = choose(near + d, w)
                for c in range(2):
                    own[w, d, c] = picked[:, c * f_dev:(c + 1) * f_dev]

    def right(u):
        return pltpu.make_async_remote_copy(
            src_ref=pout.at[pair(u)], dst_ref=pin.at[pair(u)],
            send_sem=psend.at[0], recv_sem=precv.at[u],
            device_id={"rcv": lax.rem(z + 1, nz)}, device_id_type=MESH,
        )

    def left(u):
        return pltpu.make_async_remote_copy(
            src_ref=sout.at[pair(u)], dst_ref=sin.at[pair(u)],
            send_sem=ssend.at[0], recv_sem=srecv.at[u],
            device_id={"rcv": lax.rem(z + nz - 1, nz)}, device_id_type=MESH,
        )

    def hop(u, i):
        @pl.when(z == i)
        def _():
            if i > 0:
                right(u).wait_recv()
            if i < nz - 1:
                pout[pair(u)] = own[pair(u)] + pin[pair(u)]
                right(u).start()

        @pl.when(z == nz - 1 - i)
        def _():
            if i > 0:
                left(u).wait_recv()
            if i < nz - 1:
                sout[pair(u)] = own[pair(u)] + sin[pair(u)]
                left(u).start()

    def gather_parts(u):
        c, rows = quarter(z)
        settle(part_in.at[:, :, pair(u)], rrecv.at[u])
        total = part[:, c, pair(u), rows]
        for step in range(1, nz):
            total = total + part_in[step - 1, :, pair(u)]
        whole[:, pair(u)] = total
        for k in range(half):
            cross(k, u).start()

    def pass_on(u):
        settle(fsrc.at[z, :, pair(u)], qrecv.at[u])
        for step in range(1, nz):
            share(step, u).start()

    def finish(u):
        hop(u, nz - 1)
        for w in windows(u):
            nout[w] = own[w, 1 - core] + pin[w, 1 - core] + sin[w, 1 - core]
        swap(u).start()
        for w in windows(u):
            nsrc[core, w] = own[w, core] + pin[w, core] + sin[w, core]

    def spread_all(u):
        for step in range(1, nz):
            spread(step, u).start()

    actions = {
        "spread": spread_all, "hop": hop, "gather": gather_parts, "pass": pass_on, "finish": finish, "bulk": bulk,
    }

    def run(point):
        for entry in PLAN.get(point, []):
            name, *numbers = entry.split()
            actions[name](*[int(n) for n in numbers])

    def near_sources(u):
        settle(got.at[near + 1 - core, pair(u)], nrecv.at[u])
        settle(nsrc.at[1 - core, pair(u)], wrecv.at[u])
        for wl, w in enumerate(windows(u)):
            for gl in range(half):
                srcf[wl * half + gl] = nsrc[gl, w].astype(jnp.float32)

    def far_arrival(w):
        settle(got.at[pl.ds(far, half), w], yrecv.at[w])

    def far_sources(first, count):
        for wl in range(count):
            for gl in range(half):
                for q in range(nz):
                    lo = q % cuts * rows_q
                    srcf[wl * half + gl, q // cuts, lo:lo + rows_q] = (
                        fsrc[q, gl, first + wl].astype(jnp.float32)
                    )
        for wl in range(count):
            far_arrival(first + wl)

    def correlate(base, first, count, last=False, middle=None):
        windows = [(gl, wl) for wl in range(count) for gl in range(half)]

        def accumulate(q, _):
            sources = []
            for u in range(PAIR):
                sources.append([
                    [
                        jnp.broadcast_to(
                            srcf[i, c, pl.ds(q * PAIR + u, 1), :], (16, f_dev)
                        ).astype(jnp.bfloat16)
                        for c in range(2)
                    ]
                    for i in range(len(windows))
                ])
            for lo in range(0, r_dev, 16):
                rows = slice(lo, lo + 16)
                others = [
                    [got[base + gl, first + wl, c, rows, :] for c in range(2)]
                    for gl, wl in windows
                ]
                for u in range(PAIR):
                    real, imag = [], []
                    for (sr, si), (rr, ri) in zip(sources[u], others):
                        real.append(sr * rr + si * ri)
                        imag.append(sr * ri - si * rr)
                    while len(real) > 1:
                        real = [a + b for a, b in zip(real[::2], real[1::2])]
                        imag = [a + b for a, b in zip(imag[::2], imag[1::2])]
                    for c, term in enumerate((real[0], imag[0])):
                        total = acc[q * PAIR + u, c, rows, :] + term.astype(jnp.float32)
                        if last:
                            out[q * PAIR + u, pl.ds(2 * lo + c, 16, stride=2), :] = total * scale
                        else:
                            acc[q * PAIR + u, c, rows, :] = total
            return 0

        steps = n_src // PAIR
        if middle in PLAN:
            lax.fori_loop(0, steps // 2, accumulate, 0)
            run(middle)
            lax.fori_loop(steps // 2, steps, accumulate, 0)
        else:
            lax.fori_loop(0, steps, accumulate, 0)

    for t in range(units):
        for w in windows(t):
            for h in range(2):
                load(w, h).wait()
        transform(*UNITS[t], fresh=t == 0, point=str(t))
        if t == 0:
            bulk(0)
            for w in range(early, w_dev):
                for h in range(2):
                    load(w, h).start()
        run(f"a{t}")
        select(t)
        run(f"b{t}")
    for name in ITEMS:
        u = int(name[1])
        first, count = UNITS[u]
        if name[0] == "N":
            near_sources(u)
            correlate(near, first, count, middle="h" + name)
        else:
            for step in range(1, nz):
                share_arrival(step, u)
            far_sources(first, count)
            correlate(far, first, count, u == units - 1, middle="h" + name)
        run(name)

    settle(snd.at[pl.ds(0, nw - 1)], ysend.at[0])
    settle(part_in, rsend.at[0])
    settle(whole, qsend.at[0])
    settle(part_in, gsend.at[0])
    settle(nout, wsend.at[0])

    @pl.when(z < nz - 1)
    def _():
        settle(pout, psend.at[0])

    @pl.when(z > 0)
    def _():
        settle(sout, ssend.at[0])


def body(traces, valid, src_station):
    w_dev, r_dev, samples = traces.shape
    nw, nz = lax.axis_size("win"), lax.axis_size("rcv")
    f_dev = F // nw
    n_src = src_station.shape[0]
    fits = nw == 4 and nz == 4 and w_dev == 8 and f_dev == 128
    if not fits or r_dev % 16 or n_src % 32 or samples % 512:
        return plain_body(traces, valid, src_station)
    table = jnp.asarray(quarter_table(samples, F, samples // 16))
    bf16, f32 = jnp.bfloat16, jnp.float32
    units, half, cuts = len(UNITS), nw // 2, nz // 2
    spectra = (nw, w_dev, 2, r_dev, f_dev)
    rows = (w_dev, half, 2, n_src, f_dev)
    piece = (w_dev, n_src // cuts, f_dev)
    hbm = pl.BlockSpec(memory_space=pltpu.HBM)
    dma = pltpu.SemaphoreType.DMA
    stacks = pl.pallas_call(
        functools.partial(kernel, nw, nz, w_dev, r_dev, F),
        out_shape=jax.ShapeDtypeStruct((n_src, 2 * r_dev, f_dev), f32),
        in_specs=[hbm] * 4,
        out_specs=pl.BlockSpec(memory_space=pltpu.VMEM),
        scratch_shapes=[
            pltpu.VMEM((w_dev, 2, r_dev, samples // 2), bf16),
            pltpu.VMEM((table.shape[0], samples // 2, BLOCK), bf16),
            pltpu.VMEM((MM, r_dev, 2 * F), f32),
            pltpu.VMEM(spectra, bf16),
            pltpu.VMEM(spectra, bf16),
        ] + [pltpu.VMEM(rows, bf16)] * 5 + [
            pltpu.VMEM((half, 2, w_dev, n_src, f_dev), bf16),
            pltpu.VMEM((nz - 1, half) + piece, bf16),
            pltpu.VMEM((half,) + piece, bf16),
            pltpu.VMEM((nz, half) + piece, bf16),
            pltpu.VMEM((half, w_dev, 2, n_src, f_dev), bf16),
            pltpu.VMEM((w_dev, 2, n_src, f_dev), bf16),
            pltpu.VMEM((n_src, r_dev), f32),
            pltpu.VMEM((MM * half, 2, n_src, f_dev), f32),
            pltpu.VMEM((n_src, 2, r_dev, f_dev), f32),
            pltpu.SMEM(valid.shape, jnp.int32), pltpu.SMEM(src_station.shape, jnp.int32),
            dma((w_dev, 2)), dma((table.shape[0],)), dma((2,)),
            dma((1,)), dma((w_dev,)), dma((units,)),
            dma((1,)), dma((units,)), dma((1,)), dma((units,)),
            dma((1,)), dma((units,)), dma((1,)), dma((units,)),
            dma((1,)), dma((nz - 1, units)), dma((1,)), dma((units,)),
        ],
        compiler_params=pltpu.CompilerParams(
            collective_id=0, has_side_effects=True, vmem_limit_bytes=GRANT * 1024 * 1024
        ),
    )(
        traces,
        pltpu.with_memory_space_constraint(table, pltpu.HBM),
        pltpu.with_memory_space_constraint(valid, pltpu.HBM),
        pltpu.with_memory_space_constraint(src_station, pltpu.HBM),
    )
    return stacks.reshape(n_src, r_dev, 2, f_dev)


def solution(mesh):
    return jax.shard_map(
        body,
        mesh=mesh,
        in_specs=(P("win", ("groups", "rcv"), None), P(("groups", "win")), P("groups")),
        out_specs=P(None, ("groups", "rcv"), None, "win"),
        check_vma=False,
    )
```
